32 devices in a mesh: ctx: 16 (over z, y, x), fsdp: 2 (over core).
Axes of the slice: x: 2, y: 2, z: 4, core: 2. Of those that a mesh axis runs over, the one named last changes fastest.
Arguments:
- block_input: float32 [2, 2048, 768], P('fsdp', 'ctx'), may hold values from -6 to 6
- cotangent: float32 [2, 2048, 768], P('fsdp', 'ctx'), may hold values from -6 to 6
- block_doc: int32 [2, 32], P('fsdp'), may hold values from 0 to 3, never falling along the last dimension, each value on 1 to 16 neighbouring positions
- assign: int32 [16, 2], replicated, may hold values from 0 to 31, as said below
- ln_gain: float32 [2, 768], replicated, may hold values from 0.1 to 1.9
- ln_bias: float32 [2, 768], replicated, may hold values from -3 to 3
- w_qkv: bfloat16 [768, 2304], P('fsdp'), may hold values from -2.8867513 to 2.8867513
- qv_bias: float32 [2, 768], replicated, may hold values from -2 to 2
- w_out: bfloat16 [768, 768], P('fsdp'), may hold values from -1.25 to 1.25
- res_bias: float32 [2, 768], replicated, may hold values from -2 to 2
- w_fc: bfloat16 [768, 3072], P(None, 'fsdp'), may hold values from -0.21875 to 0.21875
- fc_bias: float32 [3072], replicated, may hold values from -3 to 3
- w_proj: bfloat16 [3072, 768], P('fsdp'), may hold values from -0.109375 to 0.109375
Outputs:
- block_output: float32 [2, 2048, 768], P('fsdp', 'ctx')
- input_grad: float32 [2, 2048, 768], P('fsdp', 'ctx')
- w_qkv_grad: float32 [768, 2304], P('fsdp', 'ctx')
- w_out_grad: float32 [768, 768], P('fsdp', 'ctx')
- w_fc_grad: float32 [768, 3072], P('ctx', 'fsdp')
- w_proj_grad: float32 [3072, 768], P('fsdp', 'ctx')
- ln_gain_grad: float32 [2, 768], replicated
- ln_bias_grad: float32 [2, 768], replicated
- qv_bias_grad: float32 [2, 768], replicated
- fc_bias_grad: float32 [3072], replicated
- res_bias_grad: float32 [2, 768], replicated
The draws below stay inside these ranges and needn't reach their ends.
Inputs may be any that keep to these rules, and one draw needn't show every extreme that they name: `assign`: row c holds a block p below 16 in column 0 and its mirror 2 * 16 - 1 - p in column 1; every block of 0 to 31 stands in exactly one row. `block_doc`: along each sequence's blocks the document number never falls; each of the 4 documents holds at least one block.
All inputs are finite; a program needn't handle non-finite values.
Results may differ from the reference program's by a relative error of at most 0.015.
Values may be sent and summed in bfloat16 or wider, within the bound.
A program may use at most 192 MiB of HBM per device.

```python
import math
import jax
import jax.numpy as jnp
import numpy as np
from jax import lax

D = 768
H = 12
HD = 64
FF = 3072
BLK = 64
DOCS = 4
TOK_DEV = 128
LEN = 2048
NB = 32
SEQS = 2
N_CTX = 16


def draw_assign(key, part):
    order = jax.random.permutation(key, N_CTX).astype(jnp.int32)
    return jnp.stack([order, 2 * N_CTX - 1 - order], axis=1).astype(jnp.int32)


def draw_w_qkv(key, part):
    normal_part = jax.random.truncated_normal(key, -6.0, 6.0, (D, 3 * D), jnp.float32) * D ** (-0.5)
    return normal_part.astype(jnp.bfloat16)


def levels(key, dims, pieces, low, top_value):
    factor_of = 1.0
    for axis_at, shards_of in pieces:
        draws = jax.random.uniform(jax.random.fold_in(jax.random.fold_in(key, 6), axis_at), (shards_of,), jnp.float32, low / len(pieces), top_value / len(pieces))
        factor_of = factor_of * jnp.repeat(jnp.exp(draws), dims[axis_at] // shards_of).reshape((-1,) + (1,) * (len(dims) - 1 - axis_at))
    return factor_of


def profile(number_of, total, bound, slope):
    loads = [(1 << 20) // math.isqrt(rank ** slope) + 1 for rank in range(2, number_of + 1)]
    spare, counts = total - bound - (number_of - 1), [1] * (number_of - 1)
    while spare > 0:
        free = [i for i in range(number_of - 1) if counts[i] < bound]
        whole, remaining = sum([loads[i] for i in free]), spare
        for i in free:
            more = min(bound - counts[i], max(1, remaining * loads[i] // whole), spare)
            counts[i] = counts[i] + more
            spare = spare - more
    return np.array([bound] + counts)


def ragged(own_key, count, total, most, skew):
    if count == 2:
        one = jax.random.randint(own_key, (), max(1, total - most), min(most, total - 1) + 1)
        return jnp.stack([one, total - one])
    tallies = jnp.asarray(profile(count, total, most, skew), jnp.int32)
    twos = (count - 1) // 2
    source_of, sink = tallies[1:1 + 2 * twos:2], tallies[2:2 + 2 * twos:2]
    margin = jnp.minimum(source_of - 1, most - sink)
    moved = jax.random.randint(jax.random.fold_in(own_key, 1), (twos,), 0, 1 << 20) % (margin + 1)
    tallies = tallies.at[1:1 + 2 * twos:2].set(source_of - moved).at[2:2 + 2 * twos:2].set(sink + moved)
    return tallies[jax.random.permutation(jax.random.fold_in(own_key, 2), count)]


def noise(stream_key, shape, deviation, reach, shards=(), kind=jnp.bfloat16):
    drawn = jax.random.normal(stream_key, shape, jnp.float32) * deviation
    if len(shards) > 0:
        drawn = levels(stream_key, shape, shards, -0.22, 0.18) * drawn
    return jnp.clip(drawn, min=-reach, max=reach).astype(kind)


def setup_inputs(seed: int = 0) -> dict:
    keys = jax.random.split(jax.random.key(seed), 14)
    return {
        "block_input": noise(keys[0], (SEQS, LEN, D), 1.0, 6.0, ((0, 2), (1, 16)), jnp.float32),
        "cotangent": noise(keys[1], (SEQS, LEN, D), 1.0, 6.0, ((0, 2), (1, 16)), jnp.float32),
        "block_doc": jax.vmap(lambda own: jnp.searchsorted(jnp.cumsum(ragged(own, DOCS, NB, NB // 2, 2)), jnp.arange(NB), side="right"))(jax.random.split(keys[2], SEQS)).reshape((SEQS, NB)).astype(jnp.int32),
        "assign": draw_assign(jax.random.fold_in(keys[13], 71), 0),
        "ln_gain": jnp.clip(1.0 + 0.18 * jax.random.normal(keys[4], (2, D), jnp.float32), 0.1, 1.9),
        "ln_bias": noise(keys[5], (2, D), 0.5, 3.0, (), jnp.float32),
        "w_qkv": draw_w_qkv(jax.random.fold_in(keys[13], 71), 0),
        "qv_bias": noise(keys[7], (2, D), 0.3, 2.0, (), jnp.float32),
        "w_out": noise(keys[8], (D, D), (D // 32) ** -0.5, 1.25, ((0, 2),)),
        "res_bias": noise(keys[9], (2, D), 0.3, 2.0, (), jnp.float32),
        "w_fc": noise(keys[10], (D, FF), D ** -0.5, 0.21875, ((1, 2),)),
        "fc_bias": noise(keys[11], (FF,), 0.5, 3.0, (), jnp.float32),
        "w_proj": noise(keys[12], (FF, D), FF ** -0.5, 0.109375, ((0, 2),)),
    }


EPSILON = 1e-05

def layer_norm(values, gain, shift):
    centre = lax.optimization_barrier(jnp.mean(values, axis=-1, keepdims=True))
    centred = values - centre
    spread = lax.optimization_barrier(jnp.mean(centred * centred, axis=-1, keepdims=True))
    return centred * lax.rsqrt(spread + EPSILON) * gain + shift

def gelu_tanh(values):
    return jax.nn.gelu(values, approximate=True)

def matmul(left, right):
    return jnp.dot(left, right, preferred_element_type=jnp.float32)

def rounded(values):
    return lax.optimization_barrier(values.astype(jnp.bfloat16)).astype(jnp.float32)

def reference(block_input, cotangent, block_doc, assign, ln_gain, ln_bias, w_qkv, qv_bias, w_out, res_bias, w_fc, fc_bias, w_proj):
    score_scale = HD ** (-0.5)
    dev_group = math.gcd(4, N_CTX)
    query_rows = dev_group * TOK_DEV
    block_total = LEN // query_rows
    flat_blocks = assign.reshape(-1)
    key_block = jnp.repeat(flat_blocks, BLK)
    positions = key_block * BLK + jnp.arange(LEN, dtype=jnp.int32) % BLK

    def per_sequence(running_total, inputs):
        x_rows, cotangent_rows, doc_ids = inputs
        documents = jnp.repeat(doc_ids[flat_blocks], BLK)
        h_one = layer_norm(x_rows, ln_gain[0], ln_bias[0]).astype(jnp.bfloat16)
        qkv_rows = matmul(h_one, w_qkv)
        queries_f = rounded(qkv_rows[:, :D] + qv_bias[0])
        keys_f = rounded(qkv_rows[:, D:2 * D])
        values_f = rounded(qkv_rows[:, 2 * D:] + qv_bias[1])
        key_heads = keys_f.reshape(LEN, H, HD)
        value_heads = values_f.reshape(LEN, H, HD)

        def scores_of(number):
            row_first = number * query_rows
            query_heads = lax.dynamic_slice_in_dim(queries_f, row_first, query_rows, 0).reshape(query_rows, H, HD)
            query_pos = lax.dynamic_slice_in_dim(positions, row_first, query_rows, 0)
            query_doc = lax.dynamic_slice_in_dim(documents, row_first, query_rows, 0)
            allowed = (positions[None, :] <= query_pos[:, None]) & (documents[None, :] == query_doc[:, None])
            raw_scores = jnp.einsum('qhd,khd->hqk', query_heads, key_heads) * score_scale
            return (query_heads, jnp.where(allowed[None], raw_scores, -jnp.inf))

        def forward_block(number):
            unused, scores = scores_of(number)
            top_score = lax.optimization_barrier(jnp.max(scores, axis=-1, keepdims=True))
            log_total = top_score + jnp.log(lax.optimization_barrier(jnp.sum(jnp.exp(scores - top_score), axis=-1, keepdims=True)))
            prob_b = rounded(jnp.exp(scores - log_total))
            mixed_out = jnp.einsum('hqk,khd->qhd', prob_b, value_heads)
            return (mixed_out.reshape(query_rows, D), log_total[..., 0])
        attn_blocks, lse_blocks = lax.map(forward_block, jnp.arange(block_total, dtype=jnp.int32))
        attn_f = attn_blocks.reshape(LEN, D)
        attn_b = attn_f.astype(jnp.bfloat16)
        mid_rows = x_rows + matmul(attn_b, w_out) + res_bias[0]
        h_two = layer_norm(mid_rows, ln_gain[1], ln_bias[1]).astype(jnp.bfloat16)
        pre_act = matmul(h_two, w_fc) + fc_bias
        hidden = gelu_tanh(pre_act).astype(jnp.bfloat16)
        out_rows = mid_rows + matmul(hidden, w_proj) + res_bias[1]
        grad_out_b = cotangent_rows.astype(jnp.bfloat16)
        projection_gradient = matmul(hidden.T, grad_out_b)
        grad_hidden = matmul(grad_out_b, w_proj.T)
        preactivation_gradient = jax.vjp(gelu_tanh, pre_act)[1](grad_hidden)[0]
        grad_pre_b = preactivation_gradient.astype(jnp.bfloat16)
        expand_gradient = matmul(h_two.T, grad_pre_b)
        grad_normed = matmul(grad_pre_b, w_fc.T)
        mid_from_norm, second_norm_gain, second_norm_bias = jax.vjp(layer_norm, mid_rows, ln_gain[1], ln_bias[1])[1](grad_normed)
        middle_gradient = cotangent_rows + mid_from_norm
        grad_mid_b = middle_gradient.astype(jnp.bfloat16)
        output_gradient = matmul(attn_b.T, grad_mid_b)
        grad_attn_f = rounded(matmul(grad_mid_b, w_out.T))

        def backward_block(sums, number):
            query_heads, scores = scores_of(number)
            row_first = number * query_rows
            prob = jnp.exp(scores - lse_blocks[number][..., None])
            prob_b = rounded(prob)
            grad_heads = lax.dynamic_slice_in_dim(grad_attn_f, row_first, query_rows, 0).reshape(query_rows, H, HD)
            attn_heads = lax.dynamic_slice_in_dim(attn_f, row_first, query_rows, 0).reshape(query_rows, H, HD)
            row_delta = lax.optimization_barrier(jnp.sum(grad_heads * attn_heads, axis=-1)).T
            grad_prob = jnp.einsum('qhd,khd->hqk', grad_heads, value_heads)
            grad_score = rounded(prob * (grad_prob - row_delta[:, :, None]) * score_scale)
            query_gradient_rows = jnp.einsum('hqk,khd->qhd', grad_score, key_heads).reshape(query_rows, D)
            split_score = grad_score.reshape(H, dev_group, TOK_DEV, LEN)
            split_prob = prob_b.reshape(H, dev_group, TOK_DEV, LEN)
            split_query = query_heads.reshape(dev_group, TOK_DEV, H, HD)
            split_grad = grad_heads.reshape(dev_group, TOK_DEV, H, HD)
            key_terms = rounded(jnp.einsum('hgtk,gthd->gkhd', split_score, split_query))
            value_terms = rounded(jnp.einsum('hgtk,gthd->gkhd', split_prob, split_grad))
            key_sum = sums[0] + lax.optimization_barrier(jnp.sum(key_terms, axis=0)).reshape(LEN, D)
            value_sum = sums[1] + lax.optimization_barrier(jnp.sum(value_terms, axis=0)).reshape(LEN, D)
            return ((key_sum, value_sum), query_gradient_rows)
        zeros_pair = (jnp.zeros((LEN, D), jnp.float32), jnp.zeros((LEN, D), jnp.float32))
        (key_grad, value_gradient_rows), query_blocks = lax.scan(backward_block, zeros_pair, jnp.arange(block_total, dtype=jnp.int32))
        query_gradient_rows = query_blocks.reshape(LEN, D)
        grad_qkv_b = jnp.concatenate([query_gradient_rows, key_grad, value_gradient_rows], axis=1).astype(jnp.bfloat16)
        query_key_value_gradient = matmul(h_one.T, grad_qkv_b)
        grad_normed_one = matmul(grad_qkv_b, w_qkv.T)
        in_from_norm, first_norm_gain, first_norm_bias = jax.vjp(layer_norm, x_rows, ln_gain[0], ln_bias[0])[1](grad_normed_one)
        input_rows = middle_gradient + in_from_norm
        summand_terms = (query_key_value_gradient, output_gradient, expand_gradient, projection_gradient, jnp.stack([first_norm_gain, second_norm_gain]), jnp.stack([first_norm_bias, second_norm_bias]), jnp.stack([lax.optimization_barrier(jnp.sum(query_gradient_rows, axis=0)), lax.optimization_barrier(jnp.sum(value_gradient_rows, axis=0))]), lax.optimization_barrier(jnp.sum(preactivation_gradient, axis=0)), jnp.stack([lax.optimization_barrier(jnp.sum(middle_gradient, axis=0)), lax.optimization_barrier(jnp.sum(cotangent_rows, axis=0))]))
        updated_state = tuple((prior_state + summand_term for prior_state, summand_term in zip(running_total, summand_terms)))
        return (updated_state, (out_rows, input_rows))
    start_totals = (jnp.zeros((D, 3 * D), jnp.float32), jnp.zeros((D, D), jnp.float32), jnp.zeros((D, FF), jnp.float32), jnp.zeros((FF, D), jnp.float32), jnp.zeros((2, D), jnp.float32), jnp.zeros((2, D), jnp.float32), jnp.zeros((2, D), jnp.float32), jnp.zeros((FF,), jnp.float32), jnp.zeros((2, D), jnp.float32))
    grand, (outputs, input_grads) = lax.scan(per_sequence, start_totals, (block_input, cotangent, block_doc))
    return (outputs, input_grads, grand[0], grand[1], grand[2], grand[3], grand[4], grand[5], grand[6], grand[7], grand[8])
```

```python
import functools

import jax
import jax.numpy as jnp
from jax import lax
from jax.experimental import pallas as pl
from jax.experimental.pallas import tpu as pltpu
from jax.sharding import PartitionSpec as P

HD = 64
EPSILON = 1e-05
MASKED = -1e30
BF = jnp.bfloat16
F32 = jnp.float32


def layer_norm(values, gain, shift):
    centre = jnp.mean(values, axis=-1, keepdims=True)
    centred = values - centre
    spread = jnp.mean(centred * centred, axis=-1, keepdims=True)
    return centred * lax.rsqrt(spread + EPSILON) * gain + shift


def gelu_tanh(values):
    return jax.nn.gelu(values, approximate=True)


def dot(a, b, ca, cb):
    return lax.dot_general(a, b, (((ca,), (cb,)), ((), ())), preferred_element_type=F32)


def head_at(index, n, heads):
    return (index * heads + n - 1) // n


def owner_of(head, n, heads):
    return (head * n) // heads


def holds_head(index, n, heads):
    return owner_of(head_at(index, n, heads), n, heads) == index


def far_first(n):
    return sorted(range(1, n), key=lambda d: (-min(d, n - d), d))


def exchange_kernel(n, heads, to_heads, x_ref, o_ref, send_sem, recv_sem, own_sem):
    me = lax.axis_index("ctx")
    barrier = pltpu.get_barrier_semaphore()
    for d in range(1, n):
        pl.semaphore_signal(
            barrier,
            inc=1,
            device_id={"ctx": lax.rem(me + d, n)},
            device_id_type=pl.DeviceIdType.MESH,
        )
    pl.semaphore_wait(barrier, n - 1)

    mine = head_at(me, n, heads)
    holder = holds_head(me, n, heads)

    def copy(d):
        peer = lax.rem(me + d, n)
        return pltpu.make_async_remote_copy(
            src_ref=x_ref.at[head_at(peer, n, heads) if to_heads else peer],
            dst_ref=o_ref.at[me if to_heads else mine],
            send_sem=send_sem.at[d],
            recv_sem=recv_sem.at[d],
            device_id={"ctx": peer},
            device_id_type=pl.DeviceIdType.MESH,
        )

    def arrival(d):
        source = lax.rem(me + n - d, n)
        slot = o_ref.at[source if to_heads else head_at(source, n, heads)]
        return pltpu.make_async_remote_copy(
            src_ref=slot,
            dst_ref=slot,
            send_sem=send_sem.at[d],
            recv_sem=recv_sem.at[d],
            device_id={"ctx": source},
            device_id_type=pl.DeviceIdType.MESH,
        )

    def sends(d):
        return holds_head(lax.rem(me + d, n), n, heads) if to_heads else holder

    def receives(d):
        return holder if to_heads else holds_head(lax.rem(me + n - d, n), n, heads)

    for d in far_first(n):

        @pl.when(sends(d))
        def _():
            copy(d).start()

    @pl.when(holder)
    def _():
        own = pltpu.make_async_copy(
            x_ref.at[mine if to_heads else me], o_ref.at[me if to_heads else mine], own_sem
        )
        own.start()
        own.wait()

    for d in range(1, n):

        @pl.when(receives(d))
        def _():
            arrival(d).wait_recv()

    for d in range(1, n):

        @pl.when(sends(d))
        def _():
            copy(d).wait_send()


def exchange(x, n, heads, to_heads, number):
    out = jax.ShapeDtypeStruct((n if to_heads else heads,) + x.shape[1:], x.dtype)
    size = x.size * 2
    return pl.pallas_call(
        functools.partial(exchange_kernel, n, heads, to_heads),
        out_shape=out,
        in_specs=[pl.BlockSpec(memory_space=pltpu.VMEM)],
        out_specs=pl.BlockSpec(memory_space=pltpu.VMEM),
        scratch_shapes=[
            pltpu.SemaphoreType.DMA((n,)),
            pltpu.SemaphoreType.DMA((n,)),
            pltpu.SemaphoreType.DMA,
        ],
        cost_estimate=pl.CostEstimate(flops=0, bytes_accessed=40 * size, transcendentals=0),
        compiler_params=pltpu.CompilerParams(collective_id=number, has_side_effects=True),
    )(x)


def forward_kernel(n, tile, x_ref, kpos_ref, qpos_ref, qlow_ref, o_ref, of_ref, lse_ref, k_s, v_s):
    tok = x_ref.shape[2]
    for c in range(n):
        cols = slice(c * tok, (c + 1) * tok)
        k_s[:, cols] = x_ref[c, HD : 2 * HD, :]
        v_s[:, cols] = x_ref[c, 2 * HD :, :]
    kpos = kpos_ref[...]
    per = tile // tok
    for t in range(n // per):
        cols = slice(t * tile, (t + 1) * tile)
        q = jnp.concatenate([x_ref[t * per + i, :HD, :] for i in range(per)], axis=1)
        q = q * jnp.asarray(HD ** (-0.5), BF)
        s = dot(k_s[...], q, 0, 0)
        ok = (kpos <= qpos_ref[:, cols]) & (kpos >= qlow_ref[:, cols])
        s = jnp.where(ok, s, MASKED)
        top = jnp.max(s, axis=0, keepdims=True)
        p = jnp.exp(s - top)
        total = jnp.sum(p, axis=0, keepdims=True)
        lse_ref[:, cols] = top + jnp.log(total)
        out = dot(v_s[...], p.astype(BF), 1, 0) / total
        of_ref[:, cols] = out
        for i in range(per):
            o_ref[t * per + i] = out[:, i * tok : (i + 1) * tok].astype(BF)


class Scatter:
    def __init__(self, parts, arrive, leave, send_sem, recv_sem, bits, order):
        self.parts, self.arrive, self.leave = parts, arrive, leave
        self.send_sem, self.recv_sem = send_sem, recv_sem
        self.bits, self.order = bits, order

    def mine(self, bit):
        name, size, at = self.bits[bit]
        return (lax.axis_index(name) // (1 << at)) % 2

    def place(self, fixed, done):
        return tuple(fixed[bit] for bit in range(len(self.bits)) if bit not in done)

    def free(self, stage):
        return [bit for bit in range(len(self.bits)) if bit not in self.order[: stage + 1]]

    def copy(self, stage):
        bit = self.order[stage]
        name, size, at = self.bits[bit]
        own = self.mine(bit)
        if stage == 0:
            at_bit = [slice(None)] * len(self.bits)
            at_bit[bit] = 1 - own
            source = self.parts.at[tuple(at_bit)]
        else:
            source = self.leave[stage - 1]
        return pltpu.make_async_remote_copy(
            src_ref=source,
            dst_ref=self.arrive[stage],
            send_sem=self.send_sem.at[stage],
            recv_sem=self.recv_sem.at[stage],
            device_id={name: lax.axis_index(name) + (1 - 2 * own) * (1 << at)},
            device_id_type=pl.DeviceIdType.MESH,
        )

    def start(self, stage):
        self.copy(stage).start()

    def total(self, stage, fixed):
        value = self.parts[self.place(fixed, ())].astype(F32)
        for before in range(stage):
            value = value + self.arrive[before][self.place(fixed, self.order[: before + 1])].astype(F32)
        return value

    def combos(self, stage):
        fixed = {bit: self.mine(bit) for bit in self.order[:stage]}
        free = self.free(stage)
        for number in range(1 << len(free)):
            chosen = {bit: (number >> (len(free) - 1 - i)) & 1 for i, bit in enumerate(free)}
            yield {**fixed, **chosen}, tuple(chosen[bit] for bit in free)

    def prepare(self, stage):
        self.copy(stage - 1).wait_recv()
        bit = self.order[stage]
        for fixed, slot in self.combos(stage):
            value = self.total(stage, {**fixed, bit: 1 - self.mine(bit)})
            self.leave[stage - 1][slot + (Ellipsis,)] = value.astype(BF)

    def finish(self):
        count = len(self.order)
        self.copy(count - 1).wait_recv()
        return self.total(count, {bit: self.mine(bit) for bit in self.order})

    def drain(self):
        for stage in range(len(self.order)):
            self.copy(stage).wait_send()


def scatter_scratch(bits, rows, cols):
    count = len(bits)
    arrive = [pltpu.VMEM((2,) * (count - 1 - stage) + (rows, cols), BF) for stage in range(count)]
    leave = [pltpu.VMEM((2,) * (count - 1 - stage) + (rows, cols), BF) for stage in range(1, count)]
    return arrive + leave + [pltpu.SemaphoreType.DMA((count,))] * 2


def scatter_of(parts, scratch, bits, order):
    count = len(bits)
    return Scatter(
        parts, scratch[:count], scratch[count : 2 * count - 1], scratch[2 * count - 1], scratch[2 * count], bits, order
    )


def device_bits(n, groups):
    fsdp = [("fsdp", groups, at) for at in reversed(range(bits_of(groups)))]
    return fsdp + [("ctx", n, at) for at in reversed(range(bits_of(n)))]


def bit_order(bits, kind):
    fsdp = [i for i, bit in enumerate(bits) if bit[0] == "fsdp"]
    ctx = [i for i, bit in enumerate(bits) if bit[0] == "ctx"][::-1]
    if kind == "y":
        ctx = [ctx[1], ctx[0]] + ctx[2:]
    if kind == "z":
        ctx = ctx[2:] + ctx[:2]
    return fsdp + ctx


def greet(names):
    barrier = pltpu.get_barrier_semaphore()
    count = 0
    for peer in names:
        pl.semaphore_signal(barrier, inc=1, device_id=peer, device_id_type=pl.DeviceIdType.MESH)
        count += 1
    pl.semaphore_wait(barrier, count)


def backward_kernel(n, heads, tile, bits, orders, *refs):
    x_ref, g_ref, of_ref, lse_ref, kpos_ref, qpos_ref, qlow_ref, proj_ref, fc_ref = refs[:9]
    o_ref, proj_out, fc_out = refs[9:12]
    k_s, v_s, dk_s, dv_s, gin, d_s, g_send, g_recv, q_send, q_recv, kv_send, kv_recv = refs[12:24]
    rest = refs[24:]
    tok = x_ref.shape[2]
    scale = HD ** (-0.5)
    me = lax.axis_index("ctx")
    mine = lax.rem(head_at(me, n, heads), heads)
    holder = holds_head(me, n, heads)
    greet([{"ctx": lax.rem(me + d, n)} for d in range(1, n)])

    def g_copy(i):
        head = lax.rem(mine + i, heads)
        return owner_of(head, n, heads), pltpu.make_async_remote_copy(
            src_ref=g_ref.at[head],
            dst_ref=gin.at[me],
            send_sem=g_send.at[i],
            recv_sem=g_recv.at[me],
            device_id={"ctx": owner_of(head, n, heads)},
            device_id_type=pl.DeviceIdType.MESH,
        )

    def back_copy(c, part):
        rows = slice(0, HD) if part == 0 else slice(HD, 3 * HD)
        return pltpu.make_async_remote_copy(
            src_ref=d_s.at[c, rows],
            dst_ref=o_ref.at[mine, rows],
            send_sem=(q_send, kv_send)[part].at[c],
            recv_sem=(q_recv, kv_recv)[part].at[mine],
            device_id={"ctx": c},
            device_id_type=pl.DeviceIdType.MESH,
        )

    def landed(ref, at, sem):
        return pltpu.make_async_remote_copy(
            src_ref=ref,
            dst_ref=ref,
            send_sem=g_send.at[0],
            recv_sem=sem.at[at],
            device_id={"ctx": lax.rem(me + 1, n)},
            device_id_type=pl.DeviceIdType.MESH,
        )

    spread = sorted(range(heads), key=lambda i: -min(i, heads - i))
    for i in spread:
        target, copy = g_copy(i)

        @pl.when(target != me)
        def _():
            copy.start()

    scatters = []
    span = len(rest) // len(orders)
    for k, order in enumerate(orders):
        source = (proj_ref, fc_ref)[k % 2]
        width = source.shape[-1] // (len(orders) // 2)
        cols = slice((k // 2) * width, (k // 2 + 1) * width)
        view = source.at[(slice(None),) * (len(bits) + 1) + (cols,)]
        scatters.append(scatter_of(view, rest[k * span : (k + 1) * span], bits, order))
    for scatter in scatters:
        scatter.start(0)

    @pl.when(holder)
    def _():
        gin[me] = g_ref[mine]
        for c in range(n):
            cols = slice(c * tok, (c + 1) * tok)
            k_s[:, cols] = x_ref[c, HD : 2 * HD, :]
            v_s[:, cols] = x_ref[c, 2 * HD :, :]

    def send_back(c, part):
        @pl.when(holder & (me != c))
        def _():
            back_copy(c, part).start()

    per = tile // tok
    for t in range(n // per):

        @pl.when(holder)
        def _():
            for i in range(per):
                c = t * per + i

                @pl.when(me != c)
                def _():
                    landed(gin.at[c], c, g_recv).wait_recv()

            kpos = kpos_ref[...]
            cols = slice(t * tile, (t + 1) * tile)
            q = jnp.concatenate([x_ref[t * per + i, :HD, :] for i in range(per)], axis=1)
            q = q * jnp.asarray(scale, BF)
            g = jnp.concatenate([gin[t * per + i] for i in range(per)], axis=1)
            delta = jnp.sum(g.astype(F32) * of_ref[:, cols], axis=0, keepdims=True)
            s = dot(k_s[...], q, 0, 0)
            ok = (kpos <= qpos_ref[:, cols]) & (kpos >= qlow_ref[:, cols])
            p = jnp.exp(jnp.where(ok, s - lse_ref[:, cols], MASKED))
            dp = dot(v_s[...], g, 0, 0)
            ds = (p * (dp - delta)).astype(BF)
            dv = dot(g, p.astype(BF), 1, 1)
            dk = dot(q, ds, 1, 1)
            dq = dot(k_s[...], ds, 1, 0) * scale
            if t == 0:
                dk_s[...] = dk
                dv_s[...] = dv
            else:
                dk_s[...] += dk
                dv_s[...] += dv
            for i in range(per):
                d_s[t * per + i, :HD, :] = dq[:, i * tok : (i + 1) * tok].astype(BF)

        if t > 0:
            for i in range(per):
                send_back((t - 1) * per + i, 0)

    @pl.when(holder)
    def _():
        for c in range(n):
            cols = slice(c * tok, (c + 1) * tok)
            d_s[c, HD : 2 * HD, :] = dk_s[:, cols].astype(BF)
            d_s[c, 2 * HD :, :] = dv_s[:, cols].astype(BF)

    for i in range(per):
        send_back(n - per + i, 0)
    for c in range(n):
        send_back(c, 1)

    @pl.when(holder)
    def _():
        o_ref[mine] = d_s[me]

    for stage in range(1, len(bits)):
        for k in range(0, len(scatters), 2):
            pair = scatters[k : k + 2]
            for scatter in pair:
                scatter.prepare(stage)
            for scatter in pair:
                scatter.start(stage)
    width = proj_ref.shape[-1] // (len(orders) // 2)
    for k, scatter in enumerate(scatters):
        out = (proj_out, fc_out)[k % 2]
        out[:, (k // 2) * width : (k // 2 + 1) * width] = scatter.finish()
    for head in range(heads):

        @pl.when(me != owner_of(head, n, heads))
        def _():
            landed(o_ref.at[head, 0:HD], head, q_recv).wait_recv()
            landed(o_ref.at[head, HD : 3 * HD], head, kv_recv).wait_recv()

    for scatter in scatters:
        scatter.drain()
    for i in spread:
        target, copy = g_copy(i)

        @pl.when(target != me)
        def _():
            copy.wait_send()

    for c in range(n):

        @pl.when(holder & (me != c))
        def _():
            back_copy(c, 0).wait_send()
            back_copy(c, 1).wait_send()


def tail_kernel(n, groups, bits, orders, *refs):
    dq_ref, h_ref, w_ref, x_ref, gm_ref, gain_ref, small_ref, attn_ref = refs[:8]
    qkv_out, out_out, in_out, small_out = refs[8:12]
    dqt, qkv_parts, out_parts, sums, sums_in, sums_send, sums_recv = refs[12:19]
    rest = refs[19:]
    heads, depth, tok = dq_ref.shape
    width = w_ref.shape[0]
    share = h_ref.shape[2]
    rows = qkv_out.shape[0]
    out_rows = out_out.shape[0]
    count = len(bits)
    peers = []
    for name, size, at in bits:
        own = lax.axis_index(name)
        peers.append({name: own + (1 - 2 * ((own // (1 << at)) % 2)) * (1 << at)})
    greet(peers)

    for part in range(3):
        for head in range(heads):
            row = part * width + head * HD
            dqt[row : row + HD, :] = dq_ref[head, part * HD : (part + 1) * HD, :]

    span = 2 * count + 1
    piece = share // (len(orders) - 1)
    scatters = []
    for k, order in enumerate(orders[:-1]):
        view = qkv_parts.at[(slice(None),) * (count + 1) + (slice(k * piece, (k + 1) * piece),)]
        scatters.append(scatter_of(view, rest[k * span : (k + 1) * span], bits, order))
    scatters.append(scatter_of(out_parts, rest[-span:], bits, orders[-1]))

    def place(number):
        return tuple((number >> (count - 1 - i)) & 1 for i in range(count))

    for k in range(len(orders) - 1):
        cols = slice(k * piece, (k + 1) * piece)
        for group in range(groups):
            grad = dot(dqt[...], h_ref[group, :, cols], 1, 0).astype(BF)
            for c in range(n):
                qkv_parts[place(group * n + c) + (slice(None), cols)] = grad[c * rows : (c + 1) * rows]
        if k > 0:
            scatters[k - 1].start(0)
    grad_mid_t = jnp.transpose(gm_ref[...]).astype(BF)
    for group in range(groups):
        grad = dot(grad_mid_t, attn_ref[group * share : (group + 1) * share, :], 1, 1).astype(BF)
        for c in range(n):
            out_parts[place(group * n + c)] = grad[c * out_rows : (c + 1) * out_rows]
    scatters[-2].start(0)

    normed = jnp.transpose(dot(w_ref[...], dqt[...], 1, 0))
    scatters[-1].start(0)
    x = x_ref[...]
    gain = gain_ref[...]
    centred = x - jnp.mean(x, axis=1, keepdims=True)
    inverse = lax.rsqrt(jnp.mean(centred * centred, axis=1, keepdims=True) + EPSILON)
    hat = centred * inverse
    scaled = normed * gain
    inner = jnp.mean(scaled, axis=1, keepdims=True)
    outer = jnp.mean(scaled * hat, axis=1, keepdims=True)
    in_out[...] = gm_ref[...] + (scaled - inner - hat * outer) * inverse
    first_gain = jnp.sum(normed * hat, axis=0, keepdims=True)
    first_bias = jnp.sum(normed, axis=0, keepdims=True)
    token_sums = dot(jnp.ones((8, tok), BF), dqt[...], 1, 1)
    row = lax.broadcasted_iota(jnp.int32, small_ref.shape, 0)
    total = small_ref[...]
    for at, value in (
        (0, first_gain),
        (2, first_bias),
        (4, token_sums[0:1, :width]),
        (5, token_sums[0:1, 2 * width :]),
    ):
        total = total + jnp.where(row == at, value, 0.0)
    sums[0] = total

    def sum_copy(j):
        return pltpu.make_async_remote_copy(
            src_ref=sums.at[j],
            dst_ref=sums_in.at[j],
            send_sem=sums_send.at[j],
            recv_sem=sums_recv.at[j],
            device_id=peers[j],
            device_id_type=pl.DeviceIdType.MESH,
        )

    for stage in range(1, count):
        for k, scatter in enumerate(scatters):
            scatter.prepare(stage)
            if k == 0:
                sum_copy(stage - 1).start()
            else:
                scatters[k - 1].start(stage)
        sum_copy(stage - 1).wait_recv()
        sums[stage] = sums[stage - 1] + sums_in[stage - 1]
        scatters[-1].start(stage)
    for k, scatter in enumerate(scatters):
        if k == 0:
            qkv_out[:, 0:piece] = scatter.finish()
            sum_copy(count - 1).start()
        elif k < len(scatters) - 1:
            qkv_out[:, k * piece : (k + 1) * piece] = scatter.finish()
        else:
            out_out[...] = scatter.finish()
    sum_copy(count - 1).wait_recv()
    small_out[...] = sums[count - 1] + sums_in[count - 1]
    for scatter in scatters:
        scatter.drain()
    for j in range(count):
        sum_copy(j).wait_send()


def bits_of(n):
    return n.bit_length() - 1


def whole_specs(count):
    return [pl.BlockSpec(memory_space=pltpu.VMEM)] * count


def attention_forward(x, kpos, qpos, qlow):
    n, _, tok = x.shape
    seq = n * tok
    return pl.pallas_call(
        functools.partial(forward_kernel, n, 2 * tok),
        out_shape=(
            jax.ShapeDtypeStruct((n, HD, tok), BF),
            jax.ShapeDtypeStruct((HD, seq), F32),
            jax.ShapeDtypeStruct((1, seq), F32),
        ),
        in_specs=whole_specs(4),
        out_specs=tuple(whole_specs(3)),
        scratch_shapes=[pltpu.VMEM((HD, seq), BF)] * 2,
        cost_estimate=pl.CostEstimate(
            flops=16 * seq * seq * HD, bytes_accessed=seq * HD * 16, transcendentals=seq * seq
        ),
    )(x, kpos, qpos, qlow)


def attention_backward(x, g, attn_f, lse, kpos, qpos, qlow, proj_grad, fc_grad, heads):
    n, _, tok = x.shape
    seq = n * tok
    bits = device_bits(n, 1)
    rows, cols = proj_grad.shape[1:]
    parts = [v.reshape((2,) * len(bits) + (rows, cols)) for v in (proj_grad, fc_grad)]
    halves = 2 if cols % 256 == 0 else 1
    orders = [bit_order(bits, "x"), bit_order(bits, "y")] * halves
    scratch = []
    for _ in orders:
        scratch += scatter_scratch(bits, rows, cols // halves)
    dma = pltpu.SemaphoreType.DMA
    return pl.pallas_call(
        functools.partial(backward_kernel, n, heads, 2 * tok, bits, orders),
        out_shape=(
            jax.ShapeDtypeStruct((heads,) + x.shape[1:], BF),
            jax.ShapeDtypeStruct((rows, cols), F32),
            jax.ShapeDtypeStruct((rows, cols), F32),
        ),
        in_specs=whole_specs(9),
        out_specs=tuple(whole_specs(3)),
        scratch_shapes=[pltpu.VMEM((HD, seq), BF)] * 2
        + [pltpu.VMEM((HD, seq), F32)] * 2
        + [pltpu.VMEM((n, HD, tok), BF), pltpu.VMEM((n, 3 * HD, tok), BF)]
        + [dma((heads,)), dma((n,)), dma((n,)), dma((heads,)), dma((n,)), dma((heads,))]
        + scratch,
        cost_estimate=pl.CostEstimate(
            flops=40 * seq * seq * HD, bytes_accessed=seq * HD * 24, transcendentals=seq * seq
        ),
        compiler_params=pltpu.CompilerParams(collective_id=2, has_side_effects=True),
    )(x, g, attn_f, lse, kpos, qpos, qlow, *parts)


def tail(grad_by_head, h_one, w_full, x_rows, grad_mid, gain, small, attn_t, n, groups):
    heads, _, tok = grad_by_head.shape
    width = x_rows.shape[1]
    share = width // groups
    bits = device_bits(n, groups)
    count = len(bits)
    pieces = 3 if share % (3 * 128) == 0 else 1
    orders = [bit_order(bits, kind) for kind in ("x", "y", "z")[:pieces]] + [bit_order(bits, "z")]
    rows, out_rows = 3 * width // n, width // n
    h_parts = jnp.transpose(h_one.reshape(tok, groups, share), (1, 0, 2))
    scratch = []
    for _ in range(pieces):
        scratch += scatter_scratch(bits, rows, share // pieces)
    scratch += scatter_scratch(bits, out_rows, share)
    dma = pltpu.SemaphoreType.DMA
    return pl.pallas_call(
        functools.partial(tail_kernel, n, groups, bits, orders),
        out_shape=(
            jax.ShapeDtypeStruct((rows, share), F32),
            jax.ShapeDtypeStruct((out_rows, share), F32),
            jax.ShapeDtypeStruct((tok, width), F32),
            jax.ShapeDtypeStruct(small.shape, F32),
        ),
        in_specs=whole_specs(8),
        out_specs=tuple(whole_specs(4)),
        scratch_shapes=[
            pltpu.VMEM((3 * width, tok), BF),
            pltpu.VMEM((2,) * count + (rows, share), BF),
            pltpu.VMEM((2,) * count + (out_rows, share), BF),
            pltpu.VMEM((count,) + small.shape, F32),
            pltpu.VMEM((count,) + small.shape, F32),
            dma((count,)),
            dma((count,)),
        ]
        + scratch,
        compiler_params=pltpu.CompilerParams(collective_id=3, has_side_effects=True),
    )(grad_by_head, h_parts, w_full, x_rows, grad_mid, gain, small, attn_t)


def shift(x, d):
    n = lax.axis_size("fsdp")
    return lax.ppermute(x, "fsdp", [((i + d) % n, i) for i in range(n)])


def gather_ring(x):
    return [x] + [shift(x, d) for d in range(1, lax.axis_size("fsdp"))]


def return_ring(chunks):
    n = lax.axis_size("fsdp")
    total = chunks[0]
    for d in range(1, n):
        total = total + shift(chunks[d].astype(BF), n - d).astype(F32)
    return total


def full_rows(x):
    n = lax.axis_size("fsdp")
    me = lax.axis_index("fsdp")
    parts = gather_ring(x)
    if n == 2:
        first = me == 0
        return jnp.concatenate(
            [jnp.where(first, parts[0], parts[1]), jnp.where(first, parts[1], parts[0])], axis=0
        )
    full = jnp.zeros((n * x.shape[0],) + x.shape[1:], x.dtype)
    for d in range(n):
        full = lax.dynamic_update_slice_in_dim(full, parts[d], ((me + d) % n) * x.shape[0], 0)
    return full


def bits_of(n):
    return n.bit_length() - 1


def body(
    block_input,
    cotangent,
    block_doc,
    assign,
    ln_gain,
    ln_bias,
    w_qkv,
    qv_bias,
    w_out,
    res_bias,
    w_fc,
    fc_bias,
    w_proj,
):
    tokens = block_input.shape[1]
    width = block_input.shape[2]
    block_len = tokens // 2
    heads = width // HD
    ff_total = fc_bias.shape[0]
    ff_local = w_fc.shape[1]
    n = lax.axis_size("ctx")
    groups = lax.axis_size("fsdp")
    seq_len = n * tokens
    x_rows = block_input.reshape(tokens, width)
    cotangent_rows = cotangent.reshape(tokens, width)

    doc_ids = block_doc.reshape(-1)
    flat = assign.reshape(-1)
    low_of = jnp.sum(doc_ids[None, :] < doc_ids[:, None], axis=1).astype(jnp.int32) * block_len
    hit = flat[:, None] == jnp.arange(2 * n, dtype=jnp.int32)[None, :]
    low_rows = jnp.sum(jnp.where(hit, low_of[None, :], 0), axis=1)
    pos = (flat[:, None] * block_len + jnp.arange(block_len, dtype=jnp.int32)[None, :]).reshape(-1)
    qpos = pos.reshape(1, seq_len)
    kpos = pos.reshape(seq_len, 1)
    qlow = jnp.broadcast_to(low_rows[:, None], (2 * n, block_len)).reshape(1, seq_len)

    qkv_full = full_rows(w_qkv)
    out_full = full_rows(w_out)
    grad_out_b = cotangent_rows.astype(BF)
    grad_rows = jnp.concatenate(gather_ring(grad_out_b), axis=0)

    h_one = layer_norm(x_rows, ln_gain[0], ln_bias[0]).astype(BF)
    bias_col = jnp.concatenate([qv_bias[0], jnp.zeros((width,), F32), qv_bias[1]])
    qkv_t = (dot(qkv_full, h_one, 0, 1) + bias_col[:, None]).astype(BF)
    by_head = jnp.transpose(qkv_t.reshape(3, heads, HD, tokens), (1, 0, 2, 3)).reshape(
        heads, 3 * HD, tokens
    )
    with jax.named_scope("ex0"):
        head_in = exchange(by_head, n, heads, True, 0)
    with jax.named_scope("attf"):
        attn_out, attn_f, lse = attention_forward(head_in, kpos, qpos, qlow)
    with jax.named_scope("ex1"):
        attn_t = exchange(attn_out, n, heads, False, 1).reshape(width, tokens)

    mid_rows = x_rows + dot(attn_t, out_full, 0, 0) + res_bias[0]
    h_two = layer_norm(mid_rows, ln_gain[1], ln_bias[1]).astype(BF)
    shard_start = lax.axis_index("fsdp") * ff_local
    h_rows = jnp.concatenate(gather_ring(h_two), axis=0)
    pre_act = dot(h_rows, w_fc, 1, 0) + lax.dynamic_slice_in_dim(fc_bias, shard_start, ff_local, 0)
    hidden = gelu_tanh(pre_act).astype(BF)
    grad_hidden = dot(grad_rows, w_proj, 1, 1)
    grad_pre = jax.vjp(gelu_tanh, pre_act)[1](grad_hidden)[0]
    grad_pre_b = grad_pre.astype(BF)
    back = dot(grad_pre_b, w_fc, 1, 1)
    grad_normed = return_ring([back[d * tokens : (d + 1) * tokens] for d in range(groups)])
    mlp = dot(hidden, w_proj, 1, 0)
    mlp_out = return_ring([mlp[d * tokens : (d + 1) * tokens] for d in range(groups)])
    block_output = mid_rows + mlp_out + res_bias[1]
    fc_local = jnp.sum(grad_pre, axis=0)
    fc_bias_grad = lax.dynamic_update_slice_in_dim(
        jnp.zeros((ff_total,), F32), fc_local, shard_start, 0
    )

    mid_from_norm, second_gain, second_bias = jax.vjp(layer_norm, mid_rows, ln_gain[1], ln_bias[1])[
        1
    ](grad_normed)
    grad_mid = cotangent_rows + mid_from_norm
    grad_mid_b = grad_mid.astype(BF)
    grad_attn_t = dot(out_full, grad_mid_b, 1, 1).astype(BF).reshape(heads, HD, tokens)
    with jax.named_scope("ex2"):
        proj_grad = dot(grad_rows, hidden, 0, 0).astype(BF).reshape(n, width // n, ff_local)
    fc_grad = dot(h_rows, grad_pre_b, 0, 0).astype(BF).reshape(n, width // n, ff_local)
    grad_by_head, proj_shard, fc_shard = attention_backward(
        head_in, grad_attn_t, attn_f, lse, kpos, qpos, qlow, proj_grad, fc_grad, heads
    )
    zero = jnp.zeros((width,), F32)
    known = jnp.concatenate(
        [
            jnp.stack(
                [
                    zero,
                    second_gain,
                    zero,
                    second_bias,
                    zero,
                    zero,
                    jnp.sum(grad_mid, axis=0),
                    jnp.sum(cotangent_rows, axis=0),
                ]
            ),
            fc_bias_grad.reshape(-1, width),
        ],
        axis=0,
    )
    known = jnp.pad(known, ((0, -known.shape[0] % 8), (0, 0)))
    qkv_shard, out_shard, input_grad, small = tail(
        grad_by_head, h_one, qkv_full, x_rows, grad_mid, ln_gain[0:1], known, attn_t, n, groups
    )
    return (
        block_output.reshape(1, tokens, width),
        input_grad.reshape(1, tokens, width),
        qkv_shard.T,
        out_shard.T,
        fc_shard,
        proj_shard.T,
        small[0:2],
        small[2:4],
        small[4:6],
        small[8 : 8 + ff_total // width].reshape(ff_total),
        small[6:8],
    )


def solution(mesh):
    in_specs = (
        P("fsdp", "ctx", None),
        P("fsdp", "ctx", None),
        P("fsdp", None),
        P(),
        P(),
        P(),
        P("fsdp", None),
        P(),
        P("fsdp", None),
        P(),
        P(None, "fsdp"),
        P(),
        P("fsdp", None),
    )
    out_specs = (
        P("fsdp", "ctx", None),
        P("fsdp", "ctx", None),
        P("fsdp", "ctx"),
        P("fsdp", "ctx"),
        P("ctx", "fsdp"),
        P("fsdp", "ctx"),
        P(),
        P(),
        P(),
        P(),
        P(),
    )
    return jax.shard_map(body, mesh=mesh, in_specs=in_specs, out_specs=out_specs, check_vma=False)
```

```python
import functools

import jax
import jax.numpy as jnp
from jax import lax
from jax.experimental import pallas as pl
from jax.experimental.pallas import tpu as pltpu
from jax.sharding import PartitionSpec as P

HD = 64
EPSILON = 1e-05
MASKED = -1e30
BF = jnp.bfloat16
F32 = jnp.float32


def layer_norm(values, gain, shift):
    centre = jnp.mean(values, axis=-1, keepdims=True)
    centred = values - centre
    spread = jnp.mean(centred * centred, axis=-1, keepdims=True)
    return centred * lax.rsqrt(spread + EPSILON) * gain + shift


def gelu_tanh(values):
    return jax.nn.gelu(values, approximate=True)


def dot(a, b, ca, cb):
    return lax.dot_general(a, b, (((ca,), (cb,)), ((), ())), preferred_element_type=F32)


def head_at(index, n, heads):
    return (index * heads + n - 1) // n


def owner_of(head, n, heads):
    return (head * n) // heads


def holds_head(index, n, heads):
    return owner_of(head_at(index, n, heads), n, heads) == index


def far_first(heads):
    return sorted(range(heads), key=lambda i: -min(i, heads - i))


def landed(ref, sem, me, n):
    return pltpu.make_async_remote_copy(
        src_ref=ref,
        dst_ref=ref,
        send_sem=sem,
        recv_sem=sem,
        device_id={"ctx": lax.rem(me + 1, n)},
        device_id_type=pl.DeviceIdType.MESH,
    )


def forward_kernel(n, heads, tile, *refs):
    x_ref, kpos_ref, qpos_ref, qlow_ref, o_ref, hin, of_ref, lse_ref = refs[:8]
    k_s, v_s, o_s, kv_send, kv_recv, q_send, q_recv, b_send, b_recv = refs[8:]
    tok = x_ref.shape[2]
    me = lax.axis_index("ctx")
    mine = lax.rem(head_at(me, n, heads), heads)
    holder = holds_head(me, n, heads)
    greet([{"ctx": lax.rem(me + d, n)} for d in range(1, n)])
    parts = ((slice(HD, 3 * HD), kv_send, kv_recv), (slice(0, HD), q_send, q_recv))

    def give(i, part):
        rows, send, recv = parts[part]
        head = lax.rem(mine + i, heads)
        target = owner_of(head, n, heads)
        return target, pltpu.make_async_remote_copy(
            src_ref=x_ref.at[head, rows],
            dst_ref=hin.at[me, rows],
            send_sem=send.at[i],
            recv_sem=recv.at[me],
            device_id={"ctx": target},
            device_id_type=pl.DeviceIdType.MESH,
        )

    def back(c):
        return pltpu.make_async_remote_copy(
            src_ref=o_s.at[c],
            dst_ref=o_ref.at[mine],
            send_sem=b_send.at[c],
            recv_sem=b_recv.at[mine],
            device_id={"ctx": c},
            device_id_type=pl.DeviceIdType.MESH,
        )

    for part in range(2):
        for i in far_first(heads):
            target, copy = give(i, part)

            @pl.when(target != me)
            def _():
                copy.start()

    @pl.when(holder)
    def _():
        hin[me] = x_ref[mine]
        for c in range(n):

            @pl.when(me != c)
            def _():
                landed(hin.at[c, parts[0][0]], kv_recv.at[c], me, n).wait_recv()

            cols = slice(c * tok, (c + 1) * tok)
            k_s[:, cols] = hin[c, HD : 2 * HD, :]
            v_s[:, cols] = hin[c, 2 * HD :, :]

    def send_back(c):
        @pl.when(holder & (me != c))
        def _():
            back(c).start()

    per = tile // tok
    for t in range(n // per):

        @pl.when(holder)
        def _():
            for i in range(per):
                c = t * per + i

                @pl.when(me != c)
                def _():
                    landed(hin.at[c, parts[1][0]], q_recv.at[c], me, n).wait_recv()

            kpos = kpos_ref[...]
            cols = slice(t * tile, (t + 1) * tile)
            q = jnp.concatenate([hin[t * per + i, :HD, :] for i in range(per)], axis=1)
            q = q * jnp.asarray(HD ** (-0.5), BF)
            s = dot(k_s[...], q, 0, 0)
            ok = (kpos <= qpos_ref[:, cols]) & (kpos >= qlow_ref[:, cols])
            s = jnp.where(ok, s, MASKED)
            top = jnp.max(s, axis=0, keepdims=True)
            p = jnp.exp(s - top)
            total = jnp.sum(p, axis=0, keepdims=True)
            lse_ref[:, cols] = top + jnp.log(total)
            out = dot(v_s[...], p.astype(BF), 1, 0) / total
            for i in range(per):
                o_s[t * per + i] = out[:, i * tok : (i + 1) * tok].astype(BF)
            of_ref[:, cols] = out

        if t > 0:
            for i in range(per):
                send_back((t - 1) * per + i)

    @pl.when(holder)
    def _():
        o_ref[mine] = o_s[me]

    for i in range(per):
        send_back(n - per + i)
    for head in range(heads):

        @pl.when(me != owner_of(head, n, heads))
        def _():
            landed(o_ref.at[head], b_recv.at[head], me, n).wait_recv()

    for part in range(2):
        for i in far_first(heads):
            target, copy = give(i, part)

            @pl.when(target != me)
            def _():
                copy.wait_send()

    for c in range(n):

        @pl.when(holder & (me != c))
        def _():
            back(c).wait_send()


class Scatter:
    def __init__(self, parts, arrive, leave, send_sem, recv_sem, bits, order):
        self.parts, self.arrive, self.leave = parts, arrive, leave
        self.send_sem, self.recv_sem = send_sem, recv_sem
        self.bits, self.order = bits, order

    def mine(self, bit):
        name, size, at = self.bits[bit]
        return (lax.axis_index(name) // (1 << at)) % 2

    def place(self, fixed, done):
        return tuple(fixed[bit] for bit in range(len(self.bits)) if bit not in done)

    def free(self, stage):
        return [bit for bit in range(len(self.bits)) if bit not in self.order[: stage + 1]]

    def copy(self, stage):
        bit = self.order[stage]
        name, size, at = self.bits[bit]
        own = self.mine(bit)
        if stage == 0:
            at_bit = [slice(None)] * len(self.bits)
            at_bit[bit] = 1 - own
            source = self.parts.at[tuple(at_bit)]
        else:
            source = self.leave[stage - 1]
        return pltpu.make_async_remote_copy(
            src_ref=source,
            dst_ref=self.arrive[stage],
            send_sem=self.send_sem.at[stage],
            recv_sem=self.recv_sem.at[stage],
            device_id={name: lax.axis_index(name) + (1 - 2 * own) * (1 << at)},
            device_id_type=pl.DeviceIdType.MESH,
        )

    def start(self, stage):
        self.copy(stage).start()

    def total(self, stage, fixed):
        value = self.parts[self.place(fixed, ())].astype(F32)
        for before in range(stage):
            value = value + self.arrive[before][self.place(fixed, self.order[: before + 1])].astype(F32)
        return value

    def combos(self, stage):
        fixed = {bit: self.mine(bit) for bit in self.order[:stage]}
        free = self.free(stage)
        for number in range(1 << len(free)):
            chosen = {bit: (number >> (len(free) - 1 - i)) & 1 for i, bit in enumerate(free)}
            yield {**fixed, **chosen}, tuple(chosen[bit] for bit in free)

    def prepare(self, stage):
        self.copy(stage - 1).wait_recv()
        bit = self.order[stage]
        for fixed, slot in self.combos(stage):
            value = self.total(stage, {**fixed, bit: 1 - self.mine(bit)})
            self.leave[stage - 1][slot + (Ellipsis,)] = value.astype(BF)

    def finish(self):
        count = len(self.order)
        self.copy(count - 1).wait_recv()
        return self.total(count, {bit: self.mine(bit) for bit in self.order})

    def drain(self):
        for stage in range(len(self.order)):
            self.copy(stage).wait_send()


def scatter_scratch(bits, rows, cols):
    count = len(bits)
    arrive = [pltpu.VMEM((2,) * (count - 1 - stage) + (rows, cols), BF) for stage in range(count)]
    leave = [pltpu.VMEM((2,) * (count - 1 - stage) + (rows, cols), BF) for stage in range(1, count)]
    return arrive + leave + [pltpu.SemaphoreType.DMA((count,))] * 2


def scatter_of(parts, scratch, bits, order):
    count = len(bits)
    return Scatter(
        parts, scratch[:count], scratch[count : 2 * count - 1], scratch[2 * count - 1], scratch[2 * count], bits, order
    )


def device_bits(n, groups):
    fsdp = [("fsdp", groups, at) for at in reversed(range(bits_of(groups)))]
    return fsdp + [("ctx", n, at) for at in reversed(range(bits_of(n)))]


def bit_order(bits, kind):
    fsdp = [i for i, bit in enumerate(bits) if bit[0] == "fsdp"]
    ctx = [i for i, bit in enumerate(bits) if bit[0] == "ctx"][::-1]
    if kind == "y":
        ctx = [ctx[1], ctx[0]] + ctx[2:]
    if kind == "z":
        ctx = ctx[2:] + ctx[:2]
    return fsdp + ctx


def greet(names):
    barrier = pltpu.get_barrier_semaphore()
    count = 0
    for peer in names:
        pl.semaphore_signal(barrier, inc=1, device_id=peer, device_id_type=pl.DeviceIdType.MESH)
        count += 1
    pl.semaphore_wait(barrier, count)


def backward_kernel(n, heads, tile, bits, plan, *refs):
    x_ref, g_ref, of_ref, lse_ref, kpos_ref, qpos_ref, qlow_ref, proj_ref, fc_ref = refs[:9]
    o_ref, proj_out, fc_out = refs[9:12]
    k_s, v_s, dk_s, dv_s, gin, d_s, g_send, g_recv, q_send, q_recv, kv_send, kv_recv = refs[12:24]
    rest = refs[24:]
    tok = x_ref.shape[2]
    scale = HD ** (-0.5)
    me = lax.axis_index("ctx")
    mine = lax.rem(head_at(me, n, heads), heads)
    holder = holds_head(me, n, heads)
    greet([{"ctx": lax.rem(me + d, n)} for d in range(1, n)])

    def g_copy(i):
        head = lax.rem(mine + i, heads)
        return owner_of(head, n, heads), pltpu.make_async_remote_copy(
            src_ref=g_ref.at[head],
            dst_ref=gin.at[me],
            send_sem=g_send.at[i],
            recv_sem=g_recv.at[me],
            device_id={"ctx": owner_of(head, n, heads)},
            device_id_type=pl.DeviceIdType.MESH,
        )

    def back_copy(c, part):
        rows = slice(0, HD) if part == 0 else slice(HD, 3 * HD)
        return pltpu.make_async_remote_copy(
            src_ref=d_s.at[c, rows],
            dst_ref=o_ref.at[mine, rows],
            send_sem=(q_send, kv_send)[part].at[c],
            recv_sem=(q_recv, kv_recv)[part].at[mine],
            device_id={"ctx": c},
            device_id_type=pl.DeviceIdType.MESH,
        )

    spread = far_first(heads)
    for i in spread:
        target, copy = g_copy(i)

        @pl.when(target != me)
        def _():
            copy.start()

    scatters = []
    span = 2 * len(bits) + 1
    for k, (source, start, size, kind) in enumerate(plan):
        view = (proj_ref, fc_ref)[source].at[
            (slice(None),) * (len(bits) + 1) + (slice(start, start + size),)
        ]
        scratch = rest[k * span : (k + 1) * span]
        scatters.append(scatter_of(view, scratch, bits, bit_order(bits, kind)))

    def progress(k, stage):
        for scatter in scatters[k : k + 2]:
            scatter.prepare(stage)
        for scatter in scatters[k : k + 2]:
            scatter.start(stage)

    early = n // (tile // tok) // 2 if len(plan) > 2 else -1
    for scatter in scatters:
        scatter.start(0)

    @pl.when(holder)
    def _():
        gin[me] = g_ref[mine]
        for c in range(n):
            cols = slice(c * tok, (c + 1) * tok)
            k_s[:, cols] = x_ref[c, HD : 2 * HD, :]
            v_s[:, cols] = x_ref[c, 2 * HD :, :]

    def send_back(c, part):
        @pl.when(holder & (me != c))
        def _():
            back_copy(c, part).start()

    per = tile // tok
    for t in range(n // per):

        @pl.when(holder)
        def _():
            for i in range(per):
                c = t * per + i

                @pl.when(me != c)
                def _():
                    landed(gin.at[c], g_recv.at[c], me, n).wait_recv()

            kpos = kpos_ref[...]
            cols = slice(t * tile, (t + 1) * tile)
            q = jnp.concatenate([x_ref[t * per + i, :HD, :] for i in range(per)], axis=1)
            q = q * jnp.asarray(scale, BF)
            g = jnp.concatenate([gin[t * per + i] for i in range(per)], axis=1)
            delta = jnp.sum(g.astype(F32) * of_ref[:, cols], axis=0, keepdims=True)
            s = dot(k_s[...], q, 0, 0)
            ok = (kpos <= qpos_ref[:, cols]) & (kpos >= qlow_ref[:, cols])
            p = jnp.exp(jnp.where(ok, s - lse_ref[:, cols], MASKED))
            dp = dot(v_s[...], g, 0, 0)
            ds = (p * (dp - delta)).astype(BF)
            dv = dot(g, p.astype(BF), 1, 1)
            dk = dot(q, ds, 1, 1)
            dq = dot(k_s[...], ds, 1, 0) * scale
            if t == 0:
                dk_s[...] = dk
                dv_s[...] = dv
            else:
                dk_s[...] += dk
                dv_s[...] += dv
            for i in range(per):
                d_s[t * per + i, :HD, :] = dq[:, i * tok : (i + 1) * tok].astype(BF)

        if t > 0:
            for i in range(per):
                send_back((t - 1) * per + i, 0)
        if t == early:
            progress(2, 1)

    @pl.when(holder)
    def _():
        for c in range(n):
            cols = slice(c * tok, (c + 1) * tok)
            d_s[c, HD : 2 * HD, :] = dk_s[:, cols].astype(BF)
            d_s[c, 2 * HD :, :] = dv_s[:, cols].astype(BF)

    for i in range(per):
        send_back(n - per + i, 0)
    for c in range(n):
        send_back(c, 1)

    @pl.when(holder)
    def _():
        o_ref[mine] = d_s[me]

    count = len(bits)
    for stage in range(1, count + 1):
        for k in range(0, len(plan), 4):
            if stage < count:
                progress(k, stage)
        if len(plan) > 2 and stage + 1 < count:
            progress(2, stage + 1)
    for k, scatter in enumerate(scatters):
        source, start, size, kind = plan[k]
        (proj_out, fc_out)[source][:, start : start + size] = scatter.finish()
    for head in range(heads):

        @pl.when(me != owner_of(head, n, heads))
        def _():
            landed(o_ref.at[head, 0:HD], q_recv.at[head], me, n).wait_recv()
            landed(o_ref.at[head, HD : 3 * HD], kv_recv.at[head], me, n).wait_recv()

    for scatter in scatters:
        scatter.drain()
    for i in spread:
        target, copy = g_copy(i)

        @pl.when(target != me)
        def _():
            copy.wait_send()

    for c in range(n):

        @pl.when(holder & (me != c))
        def _():
            back_copy(c, 0).wait_send()
            back_copy(c, 1).wait_send()


def tail_kernel(n, groups, bits, orders, *refs):
    w_refs, refs = refs[:groups], refs[groups:]
    dq_ref, h_ref, x_ref, gm_ref, gain_ref, small_ref, attn_ref, proj_ref = refs[:8]
    qkv_out, out_out, in_out, small_out, proj_out = refs[8:13]
    dqt, qkv_parts, out_parts, sums, sums_in, sums_send, sums_recv, normed_s = refs[13:21]
    rest = refs[21:]
    heads, depth, tok = dq_ref.shape
    share = h_ref.shape[2]
    width = groups * share
    rows = qkv_out.shape[0]
    out_rows = out_out.shape[0]
    count = len(bits)
    peers = []
    for name, size, at in bits:
        own = lax.axis_index(name)
        peers.append({name: own + (1 - 2 * ((own // (1 << at)) % 2)) * (1 << at)})
    greet(peers)

    for part in range(3):
        for head in range(heads):
            row = part * width + head * HD
            dqt[row : row + HD, :] = dq_ref[head, part * HD : (part + 1) * HD, :]

    span = 2 * count + 1
    piece = share // (len(orders) - 1)
    scatters = []
    for k, order in enumerate(orders[:-1]):
        view = qkv_parts.at[(slice(None),) * (count + 1) + (slice(k * piece, (k + 1) * piece),)]
        scatters.append(scatter_of(view, rest[k * span : (k + 1) * span], bits, order))
    scatters.append(scatter_of(out_parts, rest[-span:], bits, orders[-1]))

    def place(number):
        return tuple((number >> (count - 1 - i)) & 1 for i in range(count))

    for k in range(len(orders) - 1):
        cols = slice(k * piece, (k + 1) * piece)
        for group in range(groups):
            grad = dot(dqt[...], h_ref[group, :, cols], 1, 0).astype(BF)
            for c in range(n):
                qkv_parts[place(group * n + c) + (slice(None), cols)] = grad[c * rows : (c + 1) * rows]
        if k > 0:
            scatters[k - 1].start(0)
    grad_mid_t = jnp.transpose(gm_ref[...]).astype(BF)
    for group in range(groups):
        grad = dot(grad_mid_t, attn_ref[group * share : (group + 1) * share, :], 1, 1).astype(BF)
        for c in range(n):
            out_parts[place(group * n + c)] = grad[c * out_rows : (c + 1) * out_rows]
    scatters[-2].start(0)

    for d in range(groups):
        row = lax.rem(lax.axis_index("fsdp") + d, groups) * share
        normed_s[pl.ds(pl.multiple_of(row, 8), share), :] = dot(w_refs[d][...], dqt[...], 1, 0)
    scatters[-1].start(0)
    normed = jnp.transpose(normed_s[...])
    x = x_ref[...]
    gain = gain_ref[...]
    centred = x - jnp.mean(x, axis=1, keepdims=True)
    inverse = lax.rsqrt(jnp.mean(centred * centred, axis=1, keepdims=True) + EPSILON)
    hat = centred * inverse
    scaled = normed * gain
    inner = jnp.mean(scaled, axis=1, keepdims=True)
    outer = jnp.mean(scaled * hat, axis=1, keepdims=True)
    in_out[...] = gm_ref[...] + (scaled - inner - hat * outer) * inverse
    first_gain = jnp.sum(normed * hat, axis=0, keepdims=True)
    first_bias = jnp.sum(normed, axis=0, keepdims=True)
    token_sums = dot(jnp.ones((8, tok), BF), dqt[...], 1, 1)
    row = lax.broadcasted_iota(jnp.int32, small_ref.shape, 0)
    total = small_ref[...]
    for at, value in (
        (0, first_gain),
        (2, first_bias),
        (4, token_sums[0:1, :width]),
        (5, token_sums[0:1, 2 * width :]),
    ):
        total = total + jnp.where(row == at, value, 0.0)
    sums[0] = total
    proj_out[...] = jnp.transpose(proj_ref[...])

    def sum_copy(j):
        return pltpu.make_async_remote_copy(
            src_ref=sums.at[j],
            dst_ref=sums_in.at[j],
            send_sem=sums_send.at[j],
            recv_sem=sums_recv.at[j],
            device_id=peers[j],
            device_id_type=pl.DeviceIdType.MESH,
        )

    for stage in range(1, count):
        for k, scatter in enumerate(scatters):
            scatter.prepare(stage)
            if k == 0:
                sum_copy(stage - 1).start()
            else:
                scatters[k - 1].start(stage)
        sum_copy(stage - 1).wait_recv()
        sums[stage] = sums[stage - 1] + sums_in[stage - 1]
        scatters[-1].start(stage)
    for k, scatter in enumerate(scatters):
        if k == 0:
            qkv_out[:, 0:piece] = scatter.finish()
            sum_copy(count - 1).start()
        elif k < len(scatters) - 1:
            qkv_out[:, k * piece : (k + 1) * piece] = scatter.finish()
        else:
            out_out[...] = scatter.finish()
    sum_copy(count - 1).wait_recv()
    small_out[...] = sums[count - 1] + sums_in[count - 1]
    for scatter in scatters:
        scatter.drain()
    for j in range(count):
        sum_copy(j).wait_send()


def bits_of(n):
    return n.bit_length() - 1


def whole_specs(count):
    return [pl.BlockSpec(memory_space=pltpu.VMEM)] * count


def attention_forward(x, kpos, qpos, qlow, n):
    heads, _, tok = x.shape
    seq = n * tok
    dma = pltpu.SemaphoreType.DMA
    return pl.pallas_call(
        functools.partial(forward_kernel, n, heads, 2 * tok),
        out_shape=(
            jax.ShapeDtypeStruct((heads, HD, tok), BF),
            jax.ShapeDtypeStruct((n,) + x.shape[1:], BF),
            jax.ShapeDtypeStruct((HD, seq), F32),
            jax.ShapeDtypeStruct((1, seq), F32),
        ),
        in_specs=whole_specs(4),
        out_specs=tuple(whole_specs(4)),
        scratch_shapes=[pltpu.VMEM((HD, seq), BF)] * 2
        + [pltpu.VMEM((n, HD, tok), BF)]
        + [dma((heads,)), dma((n,)), dma((heads,)), dma((n,)), dma((n,)), dma((heads,))],
        cost_estimate=pl.CostEstimate(
            flops=16 * seq * seq * HD, bytes_accessed=seq * HD * 16, transcendentals=seq * seq
        ),
        compiler_params=pltpu.CompilerParams(collective_id=0, has_side_effects=True),
    )(x, kpos, qpos, qlow)


def column_plan(cols):
    side = cols // 6
    rest = (cols - side) // 2
    if cols % 6 or side % 128 or rest % 128:
        return [(0, 0, cols, "x"), (1, 0, cols, "y")]
    plan = []
    for start, size, kinds in ((0, rest, "xy"), (2 * rest, side, "zz"), (rest, rest, "xy")):
        plan += [(source, start, size, kinds[source]) for source in range(2)]
    return plan


def attention_backward(x, g, attn_f, lse, kpos, qpos, qlow, proj_grad, fc_grad, heads):
    n, _, tok = x.shape
    seq = n * tok
    bits = device_bits(n, 1)
    rows, cols = proj_grad.shape[1:]
    parts = [v.reshape((2,) * len(bits) + (rows, cols)) for v in (proj_grad, fc_grad)]
    plan = column_plan(cols)
    scratch = []
    for _, _, size, _ in plan:
        scratch += scatter_scratch(bits, rows, size)
    dma = pltpu.SemaphoreType.DMA
    return pl.pallas_call(
        functools.partial(backward_kernel, n, heads, 2 * tok, bits, plan),
        out_shape=(
            jax.ShapeDtypeStruct((heads,) + x.shape[1:], BF),
            jax.ShapeDtypeStruct((rows, cols), F32),
            jax.ShapeDtypeStruct((rows, cols), F32),
        ),
        in_specs=whole_specs(9),
        out_specs=tuple(whole_specs(3)),
        scratch_shapes=[pltpu.VMEM((HD, seq), BF)] * 2
        + [pltpu.VMEM((HD, seq), F32)] * 2
        + [pltpu.VMEM((n, HD, tok), BF), pltpu.VMEM((n, 3 * HD, tok), BF)]
        + [dma((heads,)), dma((n,)), dma((n,)), dma((heads,)), dma((n,)), dma((heads,))]
        + scratch,
        cost_estimate=pl.CostEstimate(
            flops=40 * seq * seq * HD, bytes_accessed=seq * HD * 24, transcendentals=seq * seq
        ),
        compiler_params=pltpu.CompilerParams(collective_id=1, has_side_effects=True),
    )(x, g, attn_f, lse, kpos, qpos, qlow, *parts)


def tail(w_parts, grad_by_head, h_parts, x_rows, grad_mid, gain, small, attn_t, proj_shard, n):
    groups = len(w_parts)
    heads, _, tok = grad_by_head.shape
    width = x_rows.shape[1]
    share = width // groups
    bits = device_bits(n, groups)
    count = len(bits)
    pieces = 3 if share % (3 * 128) == 0 else 1
    orders = [bit_order(bits, kind) for kind in ("x", "y", "z")[:pieces]] + [bit_order(bits, "x")]
    rows, out_rows = 3 * width // n, width // n
    scratch = []
    for _ in range(pieces):
        scratch += scatter_scratch(bits, rows, share // pieces)
    scratch += scatter_scratch(bits, out_rows, share)
    dma = pltpu.SemaphoreType.DMA
    return pl.pallas_call(
        functools.partial(tail_kernel, n, groups, bits, orders),
        out_shape=(
            jax.ShapeDtypeStruct((rows, share), F32),
            jax.ShapeDtypeStruct((out_rows, share), F32),
            jax.ShapeDtypeStruct((tok, width), F32),
            jax.ShapeDtypeStruct(small.shape, F32),
            jax.ShapeDtypeStruct(proj_shard.shape[::-1], F32),
        ),
        in_specs=whole_specs(groups + 8),
        out_specs=tuple(whole_specs(5)),
        scratch_shapes=[
            pltpu.VMEM((3 * width, tok), BF),
            pltpu.VMEM((2,) * count + (rows, share), BF),
            pltpu.VMEM((2,) * count + (out_rows, share), BF),
            pltpu.VMEM((count,) + small.shape, F32),
            pltpu.VMEM((count,) + small.shape, F32),
            dma((count,)),
            dma((count,)),
            pltpu.VMEM((width, tok), F32),
        ]
        + scratch,
        compiler_params=pltpu.CompilerParams(collective_id=2, has_side_effects=True),
    )(*w_parts, grad_by_head, h_parts, x_rows, grad_mid, gain, small, attn_t, proj_shard)


def shift(x, d):
    n = lax.axis_size("fsdp")
    return lax.ppermute(x, "fsdp", [((i + d) % n, i) for i in range(n)])


def gather_ring(x):
    return [x] + [shift(x, d) for d in range(1, lax.axis_size("fsdp"))]


def return_ring(chunks):
    n = lax.axis_size("fsdp")
    total = chunks[0]
    for d in range(1, n):
        total = total + shift(chunks[d].astype(BF), n - d).astype(F32)
    return total


def in_order(parts):
    n = lax.axis_size("fsdp")
    me = lax.axis_index("fsdp")
    if n == 2:
        first = me == 0
        return jnp.concatenate(
            [jnp.where(first, parts[0], parts[1]), jnp.where(first, parts[1], parts[0])], axis=0
        )
    rows = parts[0].shape[0]
    full = jnp.zeros((n * rows,) + parts[0].shape[1:], parts[0].dtype)
    for d in range(n):
        full = lax.dynamic_update_slice_in_dim(full, parts[d], ((me + d) % n) * rows, 0)
    return full


def bias_col_of(qv_bias):
    return jnp.concatenate([qv_bias[0], jnp.zeros_like(qv_bias[0]), qv_bias[1]])


def body(
    block_input,
    cotangent,
    block_doc,
    assign,
    ln_gain,
    ln_bias,
    w_qkv,
    qv_bias,
    w_out,
    res_bias,
    w_fc,
    fc_bias,
    w_proj,
):
    tokens = block_input.shape[1]
    width = block_input.shape[2]
    block_len = tokens // 2
    heads = width // HD
    ff_total = fc_bias.shape[0]
    ff_local = w_fc.shape[1]
    n = lax.axis_size("ctx")
    groups = lax.axis_size("fsdp")
    seq_len = n * tokens
    x_rows = block_input.reshape(tokens, width)
    cotangent_rows = cotangent.reshape(tokens, width)

    doc_ids = block_doc.reshape(-1)
    flat = assign.reshape(-1)
    low_of = jnp.sum(doc_ids[None, :] < doc_ids[:, None], axis=1).astype(jnp.int32) * block_len
    hit = flat[:, None] == jnp.arange(2 * n, dtype=jnp.int32)[None, :]
    low_rows = jnp.sum(jnp.where(hit, low_of[None, :], 0), axis=1)
    pos = (flat[:, None] * block_len + jnp.arange(block_len, dtype=jnp.int32)[None, :]).reshape(-1)
    qpos = pos.reshape(1, seq_len)
    kpos = pos.reshape(seq_len, 1)
    qlow = jnp.broadcast_to(low_rows[:, None], (2 * n, block_len)).reshape(1, seq_len)

    qkv_parts = gather_ring(w_qkv)
    out_parts = gather_ring(w_out)
    share = width // groups
    owners = [lax.rem(lax.axis_index("fsdp") + d, groups) for d in range(groups)]
    grad_out_b = cotangent_rows.astype(BF)
    grad_rows = jnp.concatenate(gather_ring(grad_out_b), axis=0)

    h_one = layer_norm(x_rows, ln_gain[0], ln_bias[0]).astype(BF)
    h_parts = jnp.transpose(h_one.reshape(tokens, groups, share), (1, 0, 2))
    qkv_sum = bias_col_of(qv_bias)[:, None]
    for owner, part in zip(owners, qkv_parts):
        qkv_sum = qkv_sum + dot(part, lax.dynamic_index_in_dim(h_parts, owner, 0, False), 0, 1)
    qkv_t = qkv_sum.astype(BF)
    by_head = jnp.transpose(qkv_t.reshape(3, heads, HD, tokens), (1, 0, 2, 3)).reshape(
        heads, 3 * HD, tokens
    )
    attn_out, head_in, attn_f, lse = attention_forward(by_head, kpos, qpos, qlow, n)
    attn_t = attn_out.reshape(width, tokens)

    mid_rows = x_rows + res_bias[0]
    for owner, part in zip(owners, out_parts):
        mid_rows = mid_rows + dot(
            lax.dynamic_slice_in_dim(attn_t, owner * share, share, 0), part, 0, 0
        )
    h_two = layer_norm(mid_rows, ln_gain[1], ln_bias[1]).astype(BF)
    shard_start = lax.axis_index("fsdp") * ff_local
    h_rows = jnp.concatenate(gather_ring(h_two), axis=0)
    pre_act = dot(h_rows, w_fc, 1, 0) + lax.dynamic_slice_in_dim(fc_bias, shard_start, ff_local, 0)
    hidden = gelu_tanh(pre_act).astype(BF)
    grad_hidden = dot(grad_rows, w_proj, 1, 1)
    grad_pre = jax.vjp(gelu_tanh, pre_act)[1](grad_hidden)[0]
    grad_pre_b = grad_pre.astype(BF)
    back = dot(grad_pre_b, w_fc, 1, 1)
    grad_normed = return_ring([back[d * tokens : (d + 1) * tokens] for d in range(groups)])
    mlp = dot(hidden, w_proj, 1, 0)
    mlp_out = return_ring([mlp[d * tokens : (d + 1) * tokens] for d in range(groups)])
    block_output = mid_rows + mlp_out + res_bias[1]
    fc_local = jnp.sum(grad_pre, axis=0)
    fc_bias_grad = lax.dynamic_update_slice_in_dim(
        jnp.zeros((ff_total,), F32), fc_local, shard_start, 0
    )

    mid_from_norm, second_gain, second_bias = jax.vjp(layer_norm, mid_rows, ln_gain[1], ln_bias[1])[
        1
    ](grad_normed)
    grad_mid = cotangent_rows + mid_from_norm
    grad_mid_b = grad_mid.astype(BF)
    grad_attn_t = in_order([dot(part, grad_mid_b, 1, 1).astype(BF) for part in out_parts])
    grad_attn_t = grad_attn_t.reshape(heads, HD, tokens)
    with jax.named_scope("ex2"):
        proj_grad = dot(grad_rows, hidden, 0, 0).astype(BF).reshape(n, width // n, ff_local)
    fc_grad = dot(h_rows, grad_pre_b, 0, 0).astype(BF).reshape(n, width // n, ff_local)
    grad_by_head, proj_shard, fc_shard = attention_backward(
        head_in, grad_attn_t, attn_f, lse, kpos, qpos, qlow, proj_grad, fc_grad, heads
    )
    zero = jnp.zeros((width,), F32)
    known = jnp.concatenate(
        [
            jnp.stack(
                [
                    zero,
                    second_gain,
                    zero,
                    second_bias,
                    zero,
                    zero,
                    jnp.sum(grad_mid, axis=0),
                    jnp.sum(cotangent_rows, axis=0),
                ]
            ),
            fc_bias_grad.reshape(-1, width),
        ],
        axis=0,
    )
    known = jnp.pad(known, ((0, -known.shape[0] % 8), (0, 0)))
    qkv_shard, out_shard, input_grad, small, proj_shard = tail(
        qkv_parts,
        grad_by_head,
        h_parts,
        x_rows,
        grad_mid,
        ln_gain[0:1],
        known,
        attn_t,
        proj_shard,
        n,
    )
    return (
        block_output.reshape(1, tokens, width),
        input_grad.reshape(1, tokens, width),
        qkv_shard.T,
        out_shard.T,
        fc_shard,
        proj_shard,
        small[0:2],
        small[2:4],
        small[4:6],
        small[8 : 8 + ff_total // width].reshape(ff_total),
        small[6:8],
    )


def solution(mesh):
    in_specs = (
        P("fsdp", "ctx", None),
        P("fsdp", "ctx", None),
        P("fsdp", None),
        P(),
        P(),
        P(),
        P("fsdp", None),
        P(),
        P("fsdp", None),
        P(),
        P(None, "fsdp"),
        P(),
        P("fsdp", None),
    )
    out_specs = (
        P("fsdp", "ctx", None),
        P("fsdp", "ctx", None),
        P("fsdp", "ctx"),
        P("fsdp", "ctx"),
        P("ctx", "fsdp"),
        P("fsdp", "ctx"),
        P(),
        P(),
        P(),
        P(),
        P(),
    )
    return jax.shard_map(body, mesh=mesh, in_specs=in_specs, out_specs=out_specs, check_vma=False)
```

```python
import functools

import jax
import jax.numpy as jnp
from jax import lax
from jax.experimental import pallas as pl
from jax.experimental.pallas import tpu as pltpu
from jax.sharding import PartitionSpec as P

HD = 64
EPSILON = 1e-05
MASKED = -1e30
BF = jnp.bfloat16
F32 = jnp.float32


def layer_norm(values, gain, shift):
    centre = jnp.mean(values, axis=-1, keepdims=True)
    centred = values - centre
    spread = jnp.mean(centred * centred, axis=-1, keepdims=True)
    return centred * lax.rsqrt(spread + EPSILON) * gain + shift


def gelu_tanh(values):
    return jax.nn.gelu(values, approximate=True)


def dot(a, b, ca, cb):
    return lax.dot_general(a, b, (((ca,), (cb,)), ((), ())), preferred_element_type=F32)


def head_at(index, n, heads):
    return (index * heads + n - 1) // n


def owner_of(head, n, heads):
    return (head * n) // heads


def holds_head(index, n, heads):
    return owner_of(head_at(index, n, heads), n, heads) == index


def far_first(heads):
    return sorted(range(heads), key=lambda i: -min(i, heads - i))


def landed(ref, sem, me, n):
    return pltpu.make_async_remote_copy(
        src_ref=ref,
        dst_ref=ref,
        send_sem=sem,
        recv_sem=sem,
        device_id={"ctx": lax.rem(me + 1, n)},
        device_id_type=pl.DeviceIdType.MESH,
    )


def forward_kernel(n, groups, heads, tile, *refs):
    w_refs, refs = refs[:groups], refs[groups:]
    h_ref, bias_ref, kpos_ref, qpos_ref, qlow_ref, o_ref, hin, of_ref, lse_ref = refs[:9]
    x_s, k_s, v_s, o_s, kv_send, kv_recv, q_send, q_recv, b_send, b_recv = refs[9:]
    tok = h_ref.shape[1]
    width = heads * HD
    me = lax.axis_index("ctx")
    mine = lax.rem(head_at(me, n, heads), heads)
    holder = holds_head(me, n, heads)
    barrier = pltpu.get_barrier_semaphore()
    for d in range(1, n):
        pl.semaphore_signal(
            barrier,
            inc=1,
            device_id={"ctx": lax.rem(me + d, n)},
            device_id_type=pl.DeviceIdType.MESH,
        )
    for part in (1, 2, 0):
        cols = slice(part * width, (part + 1) * width)
        total = bias_ref[:, cols]
        for d in range(groups):
            owner = lax.rem(lax.axis_index("fsdp") + d, groups)
            total = total + dot(h_ref[owner], w_refs[d][:, cols], 1, 0)
        x_s[part] = jnp.transpose(total).astype(BF).reshape(heads, HD, tok)
    pl.semaphore_wait(barrier, n - 1)
    parts = ((slice(1, 3), kv_send, kv_recv), (slice(0, 1), q_send, q_recv))

    def give(i, part):
        rows, send, recv = parts[part]
        head = lax.rem(mine + i, heads)
        target = owner_of(head, n, heads)
        return target, pltpu.make_async_remote_copy(
            src_ref=x_s.at[rows, head],
            dst_ref=hin.at[me, rows],
            send_sem=send.at[i],
            recv_sem=recv.at[me],
            device_id={"ctx": target},
            device_id_type=pl.DeviceIdType.MESH,
        )

    def back(c):
        return pltpu.make_async_remote_copy(
            src_ref=o_s.at[c],
            dst_ref=o_ref.at[mine],
            send_sem=b_send.at[c],
            recv_sem=b_recv.at[mine],
            device_id={"ctx": c},
            device_id_type=pl.DeviceIdType.MESH,
        )

    for part in range(2):
        for i in far_first(heads):
            target, copy = give(i, part)

            @pl.when(target != me)
            def _():
                copy.start()

    @pl.when(holder)
    def _():
        hin[me] = x_s[:, mine]
        for c in range(n):

            @pl.when(me != c)
            def _():
                landed(hin.at[c, parts[0][0]], kv_recv.at[c], me, n).wait_recv()

            cols = slice(c * tok, (c + 1) * tok)
            k_s[:, cols] = hin[c, 1]
            v_s[:, cols] = hin[c, 2]

    def send_back(c):
        @pl.when(holder & (me != c))
        def _():
            back(c).start()

    per = tile // tok
    for t in range(n // per):

        @pl.when(holder)
        def _():
            for i in range(per):
                c = t * per + i

                @pl.when(me != c)
                def _():
                    landed(hin.at[c, parts[1][0]], q_recv.at[c], me, n).wait_recv()

            kpos = kpos_ref[...]
            cols = slice(t * tile, (t + 1) * tile)
            q = jnp.concatenate([hin[t * per + i, 0] for i in range(per)], axis=1)
            q = q * jnp.asarray(HD ** (-0.5), BF)
            s = dot(k_s[...], q, 0, 0)
            ok = (kpos <= qpos_ref[:, cols]) & (kpos >= qlow_ref[:, cols])
            s = jnp.where(ok, s, MASKED)
            top = jnp.max(s, axis=0, keepdims=True)
            p = jnp.exp(s - top)
            total = jnp.sum(p, axis=0, keepdims=True)
            lse_ref[:, cols] = top + jnp.log(total)
            out = dot(v_s[...], p.astype(BF), 1, 0) / total
            for i in range(per):
                o_s[t * per + i] = out[:, i * tok : (i + 1) * tok].astype(BF)
            of_ref[:, cols] = out

        if t > 0:
            for i in range(per):
                send_back((t - 1) * per + i)

    @pl.when(holder)
    def _():
        o_ref[mine] = o_s[me]

    for i in range(per):
        send_back(n - per + i)
    for head in range(heads):

        @pl.when(me != owner_of(head, n, heads))
        def _():
            landed(o_ref.at[head], b_recv.at[head], me, n).wait_recv()

    for part in range(2):
        for i in far_first(heads):
            target, copy = give(i, part)

            @pl.when(target != me)
            def _():
                copy.wait_send()

    for c in range(n):

        @pl.when(holder & (me != c))
        def _():
            back(c).wait_send()


class Scatter:
    def __init__(self, parts, arrive, leave, send_sem, recv_sem, bits, order):
        self.parts, self.arrive, self.leave = parts, arrive, leave
        self.send_sem, self.recv_sem = send_sem, recv_sem
        self.bits, self.order = bits, order

    def mine(self, bit):
        name, size, at = self.bits[bit]
        return (lax.axis_index(name) // (1 << at)) % 2

    def place(self, fixed, done):
        return tuple(fixed[bit] for bit in range(len(self.bits)) if bit not in done)

    def free(self, stage):
        return [bit for bit in range(len(self.bits)) if bit not in self.order[: stage + 1]]

    def copy(self, stage):
        bit = self.order[stage]
        name, size, at = self.bits[bit]
        own = self.mine(bit)
        if stage == 0:
            at_bit = [slice(None)] * len(self.bits)
            at_bit[bit] = 1 - own
            source = self.parts.at[tuple(at_bit)]
        else:
            source = self.leave[stage - 1]
        return pltpu.make_async_remote_copy(
            src_ref=source,
            dst_ref=self.arrive[stage],
            send_sem=self.send_sem.at[stage],
            recv_sem=self.recv_sem.at[stage],
            device_id={name: lax.axis_index(name) + (1 - 2 * own) * (1 << at)},
            device_id_type=pl.DeviceIdType.MESH,
        )

    def start(self, stage):
        self.copy(stage).start()

    def total(self, stage, fixed):
        value = self.parts[self.place(fixed, ())].astype(F32)
        for before in range(stage):
            value = value + self.arrive[before][self.place(fixed, self.order[: before + 1])].astype(F32)
        return value

    def combos(self, stage):
        fixed = {bit: self.mine(bit) for bit in self.order[:stage]}
        free = self.free(stage)
        for number in range(1 << len(free)):
            chosen = {bit: (number >> (len(free) - 1 - i)) & 1 for i, bit in enumerate(free)}
            yield {**fixed, **chosen}, tuple(chosen[bit] for bit in free)

    def prepare(self, stage):
        self.copy(stage - 1).wait_recv()
        bit = self.order[stage]
        for fixed, slot in self.combos(stage):
            value = self.total(stage, {**fixed, bit: 1 - self.mine(bit)})
            self.leave[stage - 1][slot + (Ellipsis,)] = value.astype(BF)

    def finish(self):
        count = len(self.order)
        self.copy(count - 1).wait_recv()
        return self.total(count, {bit: self.mine(bit) for bit in self.order})

    def drain(self):
        for stage in range(len(self.order)):
            self.copy(stage).wait_send()


def scatter_scratch(bits, rows, cols):
    count = len(bits)
    arrive = [pltpu.VMEM((2,) * (count - 1 - stage) + (rows, cols), BF) for stage in range(count)]
    leave = [pltpu.VMEM((2,) * (count - 1 - stage) + (rows, cols), BF) for stage in range(1, count)]
    return arrive + leave + [pltpu.SemaphoreType.DMA((count,))] * 2


def scatter_of(parts, scratch, bits, order):
    count = len(bits)
    return Scatter(
        parts, scratch[:count], scratch[count : 2 * count - 1], scratch[2 * count - 1], scratch[2 * count], bits, order
    )


def device_bits(n, groups):
    fsdp = [("fsdp", groups, at) for at in reversed(range(bits_of(groups)))]
    return fsdp + [("ctx", n, at) for at in reversed(range(bits_of(n)))]


def bit_order(bits, kind):
    fsdp = [i for i, bit in enumerate(bits) if bit[0] == "fsdp"]
    ctx = [i for i, bit in enumerate(bits) if bit[0] == "ctx"][::-1]
    if kind == "y":
        ctx = [ctx[1], ctx[0]] + ctx[2:]
    if kind == "z":
        ctx = ctx[2:] + ctx[:2]
    return fsdp + ctx


def greet(names):
    barrier = pltpu.get_barrier_semaphore()
    count = 0
    for peer in names:
        pl.semaphore_signal(barrier, inc=1, device_id=peer, device_id_type=pl.DeviceIdType.MESH)
        count += 1
    pl.semaphore_wait(barrier, count)


def backward_kernel(n, heads, tile, bits, plan, *refs):
    x_ref, g_ref, of_ref, lse_ref, kpos_ref, qpos_ref, qlow_ref, proj_ref, fc_ref = refs[:9]
    o_ref, proj_out, fc_out = refs[9:12]
    k_s, v_s, dk_s, dv_s, gin, d_s, g_send, g_recv, q_send, q_recv, kv_send, kv_recv = refs[12:24]
    rest = refs[24:]
    tok = x_ref.shape[3]
    scale = HD ** (-0.5)
    me = lax.axis_index("ctx")
    mine = lax.rem(head_at(me, n, heads), heads)
    holder = holds_head(me, n, heads)
    greet([{"ctx": lax.rem(me + d, n)} for d in range(1, n)])

    def g_copy(i):
        head = lax.rem(mine + i, heads)
        return owner_of(head, n, heads), pltpu.make_async_remote_copy(
            src_ref=g_ref.at[head],
            dst_ref=gin.at[me],
            send_sem=g_send.at[i],
            recv_sem=g_recv.at[me],
            device_id={"ctx": owner_of(head, n, heads)},
            device_id_type=pl.DeviceIdType.MESH,
        )

    def back_copy(c, part):
        rows = slice(0, HD) if part == 0 else slice(HD, 3 * HD)
        return pltpu.make_async_remote_copy(
            src_ref=d_s.at[c, rows],
            dst_ref=o_ref.at[mine, rows],
            send_sem=(q_send, kv_send)[part].at[c],
            recv_sem=(q_recv, kv_recv)[part].at[mine],
            device_id={"ctx": c},
            device_id_type=pl.DeviceIdType.MESH,
        )

    spread = far_first(heads)
    for i in spread:
        target, copy = g_copy(i)

        @pl.when(target != me)
        def _():
            copy.start()

    scatters = []
    span = 2 * len(bits) + 1
    for k, (source, start, size, kind) in enumerate(plan):
        view = (proj_ref, fc_ref)[source].at[
            (slice(None),) * (len(bits) + 1) + (slice(start, start + size),)
        ]
        scratch = rest[k * span : (k + 1) * span]
        scatters.append(scatter_of(view, scratch, bits, bit_order(bits, kind)))

    def progress(k, stage):
        for scatter in scatters[k : k + 2]:
            scatter.prepare(stage)
        for scatter in scatters[k : k + 2]:
            scatter.start(stage)

    early = n // (tile // tok) // 2 if len(plan) > 2 else -1
    for scatter in scatters:
        scatter.start(0)

    @pl.when(holder)
    def _():
        gin[me] = g_ref[mine]
        for c in range(n):
            cols = slice(c * tok, (c + 1) * tok)
            k_s[:, cols] = x_ref[c, 1]
            v_s[:, cols] = x_ref[c, 2]

    def send_back(c, part):
        @pl.when(holder & (me != c))
        def _():
            back_copy(c, part).start()

    per = tile // tok
    for t in range(n // per):

        @pl.when(holder)
        def _():
            for i in range(per):
                c = t * per + i

                @pl.when(me != c)
                def _():
                    landed(gin.at[c], g_recv.at[c], me, n).wait_recv()

            kpos = kpos_ref[...]
            cols = slice(t * tile, (t + 1) * tile)
            q = jnp.concatenate([x_ref[t * per + i, 0] for i in range(per)], axis=1)
            q = q * jnp.asarray(scale, BF)
            g = jnp.concatenate([gin[t * per + i] for i in range(per)], axis=1)
            delta = jnp.sum(g.astype(F32) * of_ref[:, cols], axis=0, keepdims=True)
            s = dot(k_s[...], q, 0, 0)
            ok = (kpos <= qpos_ref[:, cols]) & (kpos >= qlow_ref[:, cols])
            p = jnp.exp(jnp.where(ok, s - lse_ref[:, cols], MASKED))
            dp = dot(v_s[...], g, 0, 0)
            ds = (p * (dp - delta)).astype(BF)
            dv = dot(g, p.astype(BF), 1, 1)
            dk = dot(q, ds, 1, 1)
            dq = dot(k_s[...], ds, 1, 0) * scale
            if t == 0:
                dk_s[...] = dk
                dv_s[...] = dv
            else:
                dk_s[...] += dk
                dv_s[...] += dv
            for i in range(per):
                d_s[t * per + i, :HD, :] = dq[:, i * tok : (i + 1) * tok].astype(BF)

        if t > 0:
            for i in range(per):
                send_back((t - 1) * per + i, 0)
        if t == early:
            progress(2, 1)

    @pl.when(holder)
    def _():
        for c in range(n):
            cols = slice(c * tok, (c + 1) * tok)
            d_s[c, HD : 2 * HD, :] = dk_s[:, cols].astype(BF)
            d_s[c, 2 * HD :, :] = dv_s[:, cols].astype(BF)

    for i in range(per):
        send_back(n - per + i, 0)
    for c in range(n):
        send_back(c, 1)

    @pl.when(holder)
    def _():
        o_ref[mine] = d_s[me]

    count = len(bits)
    for stage in range(1, count + 1):
        for k in range(0, len(plan), 4):
            if stage < count:
                progress(k, stage)
        if len(plan) > 2 and stage + 1 < count:
            progress(2, stage + 1)
    for k, scatter in enumerate(scatters):
        source, start, size, kind = plan[k]
        (proj_out, fc_out)[source][:, start : start + size] = scatter.finish()
    for head in range(heads):

        @pl.when(me != owner_of(head, n, heads))
        def _():
            landed(o_ref.at[head, 0:HD], q_recv.at[head], me, n).wait_recv()
            landed(o_ref.at[head, HD : 3 * HD], kv_recv.at[head], me, n).wait_recv()

    for scatter in scatters:
        scatter.drain()
    for i in spread:
        target, copy = g_copy(i)

        @pl.when(target != me)
        def _():
            copy.wait_send()

    for c in range(n):

        @pl.when(holder & (me != c))
        def _():
            back_copy(c, 0).wait_send()
            back_copy(c, 1).wait_send()


def tail_kernel(n, groups, bits, orders, *refs):
    w_refs, refs = refs[:groups], refs[groups:]
    dq_ref, h_ref, x_ref, gm_ref, gain_ref, small_ref, attn_ref = refs[:7]
    qkv_out, out_out, in_out, small_out = refs[7:11]
    dqt, qkv_parts, out_parts, sums, sums_in, sums_send, sums_recv, normed_s = refs[11:19]
    rest = refs[19:]
    heads, depth, tok = dq_ref.shape
    share = h_ref.shape[2]
    width = groups * share
    rows = qkv_out.shape[0]
    out_rows = out_out.shape[0]
    count = len(bits)
    peers = []
    for name, size, at in bits:
        own = lax.axis_index(name)
        peers.append({name: own + (1 - 2 * ((own // (1 << at)) % 2)) * (1 << at)})
    greet(peers)

    for part in range(3):
        for head in range(heads):
            row = part * width + head * HD
            dqt[row : row + HD, :] = dq_ref[head, part * HD : (part + 1) * HD, :]

    span = 2 * count + 1
    piece = share // (len(orders) - 1)
    scatters = []
    for k, order in enumerate(orders[:-1]):
        view = qkv_parts.at[(slice(None),) * (count + 1) + (slice(k * piece, (k + 1) * piece),)]
        scatters.append(scatter_of(view, rest[k * span : (k + 1) * span], bits, order))
    scatters.append(scatter_of(out_parts, rest[-span:], bits, orders[-1]))

    def place(number):
        return tuple((number >> (count - 1 - i)) & 1 for i in range(count))

    for k in range(len(orders) - 1):
        cols = slice(k * piece, (k + 1) * piece)
        for group in range(groups):
            grad = dot(dqt[...], h_ref[group, :, cols], 1, 0).astype(BF)
            for c in range(n):
                qkv_parts[place(group * n + c) + (slice(None), cols)] = grad[c * rows : (c + 1) * rows]
        if k > 0:
            scatters[k - 1].start(0)
    grad_mid_t = jnp.transpose(gm_ref[...]).astype(BF)
    for group in range(groups):
        grad = dot(grad_mid_t, attn_ref[group * share : (group + 1) * share, :], 1, 1).astype(BF)
        for c in range(n):
            out_parts[place(group * n + c)] = grad[c * out_rows : (c + 1) * out_rows]
    scatters[-2].start(0)

    for d in range(groups):
        row = lax.rem(lax.axis_index("fsdp") + d, groups) * share
        normed_s[pl.ds(pl.multiple_of(row, 8), share), :] = dot(w_refs[d][...], dqt[...], 1, 0)
    scatters[-1].start(0)
    normed = jnp.transpose(normed_s[...])
    x = x_ref[...]
    gain = gain_ref[...]
    centred = x - jnp.mean(x, axis=1, keepdims=True)
    inverse = lax.rsqrt(jnp.mean(centred * centred, axis=1, keepdims=True) + EPSILON)
    hat = centred * inverse
    scaled = normed * gain
    inner = jnp.mean(scaled, axis=1, keepdims=True)
    outer = jnp.mean(scaled * hat, axis=1, keepdims=True)
    in_out[...] = gm_ref[...] + (scaled - inner - hat * outer) * inverse
    first_gain = jnp.sum(normed * hat, axis=0, keepdims=True)
    first_bias = jnp.sum(normed, axis=0, keepdims=True)
    token_sums = dot(jnp.ones((8, tok), BF), dqt[...], 1, 1)
    row = lax.broadcasted_iota(jnp.int32, small_ref.shape, 0)
    total = small_ref[...]
    for at, value in (
        (0, first_gain),
        (2, first_bias),
        (4, token_sums[0:1, :width]),
        (5, token_sums[0:1, 2 * width :]),
    ):
        total = total + jnp.where(row == at, value, 0.0)
    sums[0] = total

    def sum_copy(j):
        return pltpu.make_async_remote_copy(
            src_ref=sums.at[j],
            dst_ref=sums_in.at[j],
            send_sem=sums_send.at[j],
            recv_sem=sums_recv.at[j],
            device_id=peers[j],
            device_id_type=pl.DeviceIdType.MESH,
        )

    for stage in range(1, count):
        for k, scatter in enumerate(scatters):
            scatter.prepare(stage)
            if k == 0:
                sum_copy(stage - 1).start()
            else:
                scatters[k - 1].start(stage)
        sum_copy(stage - 1).wait_recv()
        sums[stage] = sums[stage - 1] + sums_in[stage - 1]
        scatters[-1].start(stage)
    for k, scatter in enumerate(scatters):
        if k == 0:
            qkv_out[:, 0:piece] = scatter.finish()
            sum_copy(count - 1).start()
        elif k < len(scatters) - 1:
            qkv_out[:, k * piece : (k + 1) * piece] = scatter.finish()
        else:
            out_out[...] = scatter.finish()
    sum_copy(count - 1).wait_recv()
    small_out[...] = sums[count - 1] + sums_in[count - 1]
    for scatter in scatters:
        scatter.drain()
    for j in range(count):
        sum_copy(j).wait_send()


def bits_of(n):
    return n.bit_length() - 1


def whole_specs(count):
    return [pl.BlockSpec(memory_space=pltpu.VMEM)] * count


def attention_forward(w_parts, h_parts, bias, kpos, qpos, qlow, n):
    groups, tok, share = h_parts.shape
    heads = groups * share // HD
    seq = n * tok
    dma = pltpu.SemaphoreType.DMA
    return pl.pallas_call(
        functools.partial(forward_kernel, n, groups, heads, 2 * tok),
        out_shape=(
            jax.ShapeDtypeStruct((heads, HD, tok), BF),
            jax.ShapeDtypeStruct((n, 3, HD, tok), BF),
            jax.ShapeDtypeStruct((HD, seq), F32),
            jax.ShapeDtypeStruct((1, seq), F32),
        ),
        in_specs=whole_specs(groups + 5),
        out_specs=tuple(whole_specs(4)),
        scratch_shapes=[pltpu.VMEM((3, heads, HD, tok), BF)]
        + [pltpu.VMEM((HD, seq), BF)] * 2
        + [pltpu.VMEM((n, HD, tok), BF)]
        + [dma((heads,)), dma((n,)), dma((heads,)), dma((n,)), dma((n,)), dma((heads,))],
        cost_estimate=pl.CostEstimate(
            flops=16 * seq * seq * HD, bytes_accessed=seq * HD * 16, transcendentals=seq * seq
        ),
        compiler_params=pltpu.CompilerParams(collective_id=0, has_side_effects=True),
    )(*w_parts, h_parts, bias, kpos, qpos, qlow)


def column_plan(cols):
    side = cols // 6
    rest = (cols - side) // 2
    if cols % 6 or side % 128 or rest % 128:
        return [(0, 0, cols, "x"), (1, 0, cols, "y")]
    plan = []
    for start, size, kinds in ((0, rest, "xy"), (2 * rest, side, "zz"), (rest, rest, "xy")):
        plan += [(source, start, size, kinds[source]) for source in range(2)]
    return plan


def attention_backward(x, g, attn_f, lse, kpos, qpos, qlow, proj_grad, fc_grad, heads):
    n, _, _, tok = x.shape
    seq = n * tok
    bits = device_bits(n, 1)
    rows, cols = proj_grad.shape[1:]
    parts = [v.reshape((2,) * len(bits) + (rows, cols)) for v in (proj_grad, fc_grad)]
    plan = column_plan(cols)
    scratch = []
    for _, _, size, _ in plan:
        scratch += scatter_scratch(bits, rows, size)
    dma = pltpu.SemaphoreType.DMA
    return pl.pallas_call(
        functools.partial(backward_kernel, n, heads, 2 * tok, bits, plan),
        out_shape=(
            jax.ShapeDtypeStruct((heads, 3 * HD, tok), BF),
            jax.ShapeDtypeStruct((rows, cols), F32),
            jax.ShapeDtypeStruct((rows, cols), F32),
        ),
        in_specs=whole_specs(9),
        out_specs=tuple(whole_specs(3)),
        scratch_shapes=[pltpu.VMEM((HD, seq), BF)] * 2
        + [pltpu.VMEM((HD, seq), F32)] * 2
        + [pltpu.VMEM((n, HD, tok), BF), pltpu.VMEM((n, 3 * HD, tok), BF)]
        + [dma((heads,)), dma((n,)), dma((n,)), dma((heads,)), dma((n,)), dma((heads,))]
        + scratch,
        cost_estimate=pl.CostEstimate(
            flops=40 * seq * seq * HD, bytes_accessed=seq * HD * 24, transcendentals=seq * seq
        ),
        compiler_params=pltpu.CompilerParams(collective_id=1, has_side_effects=True),
    )(x, g, attn_f, lse, kpos, qpos, qlow, *parts)


def tail(w_parts, grad_by_head, h_parts, x_rows, grad_mid, gain, small, attn_t, n):
    groups = len(w_parts)
    heads, _, tok = grad_by_head.shape
    width = x_rows.shape[1]
    share = width // groups
    bits = device_bits(n, groups)
    count = len(bits)
    pieces = 3 if share % (3 * 128) == 0 else 1
    orders = [bit_order(bits, kind) for kind in ("x", "y", "z")[:pieces]] + [bit_order(bits, "x")]
    rows, out_rows = 3 * width // n, width // n
    scratch = []
    for _ in range(pieces):
        scratch += scatter_scratch(bits, rows, share // pieces)
    scratch += scatter_scratch(bits, out_rows, share)
    dma = pltpu.SemaphoreType.DMA
    return pl.pallas_call(
        functools.partial(tail_kernel, n, groups, bits, orders),
        out_shape=(
            jax.ShapeDtypeStruct((rows, share), F32),
            jax.ShapeDtypeStruct((out_rows, share), F32),
            jax.ShapeDtypeStruct((tok, width), F32),
            jax.ShapeDtypeStruct(small.shape, F32),
        ),
        in_specs=whole_specs(groups + 7),
        out_specs=tuple(whole_specs(4)),
        scratch_shapes=[
            pltpu.VMEM((3 * width, tok), BF),
            pltpu.VMEM((2,) * count + (rows, share), BF),
            pltpu.VMEM((2,) * count + (out_rows, share), BF),
            pltpu.VMEM((count,) + small.shape, F32),
            pltpu.VMEM((count,) + small.shape, F32),
            dma((count,)),
            dma((count,)),
            pltpu.VMEM((width, tok), F32),
        ]
        + scratch,
        compiler_params=pltpu.CompilerParams(collective_id=2, has_side_effects=True),
    )(*w_parts, grad_by_head, h_parts, x_rows, grad_mid, gain, small, attn_t)


def shift(x, d):
    n = lax.axis_size("fsdp")
    return lax.ppermute(x, "fsdp", [((i + d) % n, i) for i in range(n)])


def gather_ring(x):
    return [x] + [shift(x, d) for d in range(1, lax.axis_size("fsdp"))]


def return_ring(chunks):
    n = lax.axis_size("fsdp")
    total = chunks[0]
    for d in range(1, n):
        total = total + shift(chunks[d].astype(BF), n - d).astype(F32)
    return total


def in_order(parts):
    n = lax.axis_size("fsdp")
    me = lax.axis_index("fsdp")
    if n == 2:
        first = me == 0
        return jnp.concatenate(
            [jnp.where(first, parts[0], parts[1]), jnp.where(first, parts[1], parts[0])], axis=0
        )
    rows = parts[0].shape[0]
    full = jnp.zeros((n * rows,) + parts[0].shape[1:], parts[0].dtype)
    for d in range(n):
        full = lax.dynamic_update_slice_in_dim(full, parts[d], ((me + d) % n) * rows, 0)
    return full


def bias_of(qv_bias):
    return jnp.concatenate([qv_bias[0], jnp.zeros_like(qv_bias[0]), qv_bias[1]])


def body(
    block_input,
    cotangent,
    block_doc,
    assign,
    ln_gain,
    ln_bias,
    w_qkv,
    qv_bias,
    w_out,
    res_bias,
    w_fc,
    fc_bias,
    w_proj,
):
    tokens = block_input.shape[1]
    width = block_input.shape[2]
    block_len = tokens // 2
    heads = width // HD
    ff_total = fc_bias.shape[0]
    ff_local = w_fc.shape[1]
    n = lax.axis_size("ctx")
    groups = lax.axis_size("fsdp")
    seq_len = n * tokens
    x_rows = block_input.reshape(tokens, width)
    cotangent_rows = cotangent.reshape(tokens, width)

    doc_ids = block_doc.reshape(-1)
    flat = assign.reshape(-1)
    low_of = jnp.sum(doc_ids[None, :] < doc_ids[:, None], axis=1).astype(jnp.int32) * block_len
    hit = flat[:, None] == jnp.arange(2 * n, dtype=jnp.int32)[None, :]
    low_rows = jnp.sum(jnp.where(hit, low_of[None, :], 0), axis=1)
    pos = (flat[:, None] * block_len + jnp.arange(block_len, dtype=jnp.int32)[None, :]).reshape(-1)
    qpos = pos.reshape(1, seq_len)
    kpos = pos.reshape(seq_len, 1)
    qlow = jnp.broadcast_to(low_rows[:, None], (2 * n, block_len)).reshape(1, seq_len)

    qkv_parts = gather_ring(w_qkv)
    out_parts = gather_ring(w_out)
    share = width // groups
    owners = [lax.rem(lax.axis_index("fsdp") + d, groups) for d in range(groups)]
    grad_out_b = cotangent_rows.astype(BF)
    grad_rows = jnp.concatenate(gather_ring(grad_out_b), axis=0)

    h_one = layer_norm(x_rows, ln_gain[0], ln_bias[0]).astype(BF)
    h_parts = jnp.transpose(h_one.reshape(tokens, groups, share), (1, 0, 2))
    attn_out, head_in, attn_f, lse = attention_forward(
        qkv_parts, h_parts, bias_of(qv_bias)[None, :], kpos, qpos, qlow, n
    )
    attn_t = attn_out.reshape(width, tokens)

    mid_rows = x_rows + res_bias[0]
    for owner, part in zip(owners, out_parts):
        mid_rows = mid_rows + dot(
            lax.dynamic_slice_in_dim(attn_t, owner * share, share, 0), part, 0, 0
        )
    h_two = layer_norm(mid_rows, ln_gain[1], ln_bias[1]).astype(BF)
    shard_start = lax.axis_index("fsdp") * ff_local
    h_rows = jnp.concatenate(gather_ring(h_two), axis=0)
    pre_act = dot(h_rows, w_fc, 1, 0) + lax.dynamic_slice_in_dim(fc_bias, shard_start, ff_local, 0)
    hidden = gelu_tanh(pre_act).astype(BF)
    grad_hidden = dot(grad_rows, w_proj, 1, 1)
    grad_pre = jax.vjp(gelu_tanh, pre_act)[1](grad_hidden)[0]
    grad_pre_b = grad_pre.astype(BF)
    back = dot(grad_pre_b, w_fc, 1, 1)
    grad_normed = return_ring([back[d * tokens : (d + 1) * tokens] for d in range(groups)])
    mlp = dot(hidden, w_proj, 1, 0)
    mlp_out = return_ring([mlp[d * tokens : (d + 1) * tokens] for d in range(groups)])
    block_output = mid_rows + mlp_out + res_bias[1]
    fc_local = jnp.sum(grad_pre, axis=0)
    fc_bias_grad = lax.dynamic_update_slice_in_dim(
        jnp.zeros((ff_total,), F32), fc_local, shard_start, 0
    )

    mid_from_norm, second_gain, second_bias = jax.vjp(layer_norm, mid_rows, ln_gain[1], ln_bias[1])[
        1
    ](grad_normed)
    grad_mid = cotangent_rows + mid_from_norm
    grad_mid_b = grad_mid.astype(BF)
    grad_attn_t = in_order([dot(part, grad_mid_b, 1, 1).astype(BF) for part in out_parts])
    grad_attn_t = grad_attn_t.reshape(heads, HD, tokens)
    with jax.named_scope("ex2"):
        proj_grad = dot(grad_rows, hidden, 0, 0).astype(BF).reshape(n, width // n, ff_local)
    fc_grad = dot(h_rows, grad_pre_b, 0, 0).astype(BF).reshape(n, width // n, ff_local)
    grad_by_head, proj_shard, fc_shard = attention_backward(
        head_in, grad_attn_t, attn_f, lse, kpos, qpos, qlow, proj_grad, fc_grad, heads
    )
    zero = jnp.zeros((width,), F32)
    known = jnp.concatenate(
        [
            jnp.stack(
                [
                    zero,
                    second_gain,
                    zero,
                    second_bias,
                    zero,
                    zero,
                    jnp.sum(grad_mid, axis=0),
                    jnp.sum(cotangent_rows, axis=0),
                ]
            ),
            fc_bias_grad.reshape(-1, width),
        ],
        axis=0,
    )
    known = jnp.pad(known, ((0, -known.shape[0] % 8), (0, 0)))
    qkv_shard, out_shard, input_grad, small = tail(
        qkv_parts,
        grad_by_head,
        h_parts,
        x_rows,
        grad_mid,
        ln_gain[0:1],
        known,
        attn_t,
        n,
    )
    return (
        block_output.reshape(1, tokens, width),
        input_grad.reshape(1, tokens, width),
        qkv_shard.T,
        out_shard.T,
        fc_shard,
        proj_shard.T,
        small[0:2],
        small[2:4],
        small[4:6],
        small[8 : 8 + ff_total // width].reshape(ff_total),
        small[6:8],
    )


def solution(mesh):
    in_specs = (
        P("fsdp", "ctx", None),
        P("fsdp", "ctx", None),
        P("fsdp", None),
        P(),
        P(),
        P(),
        P("fsdp", None),
        P(),
        P("fsdp", None),
        P(),
        P(None, "fsdp"),
        P(),
        P("fsdp", None),
    )
    out_specs = (
        P("fsdp", "ctx", None),
        P("fsdp", "ctx", None),
        P("fsdp", "ctx"),
        P("fsdp", "ctx"),
        P("ctx", "fsdp"),
        P("fsdp", "ctx"),
        P(),
        P(),
        P(),
        P(),
        P(),
    )
    return jax.shard_map(body, mesh=mesh, in_specs=in_specs, out_specs=out_specs, check_vma=False)
```
